128 devices in a mesh: row: 8 (over x_lo, y), col: 16 (over z, x_hi, core).
Axes of the slice: x: 4 (x_hi: 2, x_lo: 2; x = x_hi * 2 + x_lo), y: 4, z: 4, core: 2. Of those that a mesh axis runs over, the one named last changes fastest.
Arguments:
- features: bfloat16 [65536, 256], P(('row', 'col')), may hold values from -6 to 6
- weight: bfloat16 [256, 256], replicated, may hold values from -0.375 to 0.375
- adjacency: bfloat16 [8, 16, 384, 128, 128], P('row', 'col'), may hold values from -0.0546875 to 0.0546875
- block_rows: int32 [8, 16, 384], P('row', 'col'), may hold values from 0 to 63
- block_cols: int32 [8, 16, 384], P('row', 'col'), may hold values from 0 to 31
- live_blocks: int32 [8, 16], P('row', 'col'), may hold values from 96 to 384, as said below
- part_gains: float32 [64, 256], replicated, may hold values from 0.5 to 2
- partition: int32 [65536], P(('row', 'col')), may hold values from 0 to 63, never falling along the last dimension, each value on 1 to 2048 neighbouring positions
- cotangent: bfloat16 [65536, 256], P(('row', 'col')), may hold values from -6 to 6
Outputs:
- layer_out: bfloat16 [65536, 256], P(('row', 'col'))
- feature_grad: bfloat16 [65536, 256], P(('row', 'col'))
- weight_grad: float32 [256, 256], replicated
- gain_grad: float32 [64, 256], replicated
The draws below stay inside these ranges and needn't reach their ends.
Inputs may be any that keep to these rules, and one draw needn't show every extreme that they name: Only the first live_blocks[i, j] slots of tile (i, j) are used; some tile uses all 384 slots. partition numbers never fall along the nodes; every partition has 1 to 2048 nodes, one exactly that many.
All inputs are finite; a program needn't handle non-finite values.
Results may differ from the reference program's by a relative error of at most 0.024.
Values may be sent and summed in bfloat16 or wider, within the bound.
A program may use at most 128 MiB of HBM per device.

```python
import math
import jax
import jax.numpy as jnp
import numpy as np
from jax import lax

WIDTH = 256
BLOCK = 128
NODE_DEV = 512
SLOTS = 384
GRID_ROWS = 8
GRID_COLS = 16
NODES = 65536
ROW_BLOCKS = 64
COL_BLOCKS = 32
PARTS_SIZE = 64


def draw_live_blocks(key, part):
    first_key, second_key = jax.random.split(jax.random.fold_in(key, 7))
    tile_total = GRID_ROWS * GRID_COLS
    drawn = jax.random.randint(first_key, (tile_total,), SLOTS // 4, SLOTS + 1)
    chosen = jax.random.randint(second_key, (), 0, tile_total)
    filled = jnp.where(jnp.arange(tile_total) == chosen, SLOTS, drawn)
    return filled.reshape(GRID_ROWS, GRID_COLS).astype(jnp.int32)


def set_ends(array, key, least, high):
    index_at = [jax.random.randint(jax.random.fold_in(key, axis), (), 0, length) for axis, length in enumerate(array.shape)]
    main_axis = array.shape.index(max(array.shape))
    next_to = index_at[:main_axis] + [(index_at[main_axis] + 1) % array.shape[main_axis]] + index_at[main_axis + 1:]
    return array.at[tuple(index_at)].set(least).at[tuple(next_to)].set(high)


def levels(stream_key, dims, pieces, low, high):
    factor_of, own = 1.0, jax.random.fold_in(stream_key, 6)
    for axis_at, parts in pieces:
        steps = jnp.exp(jax.random.uniform(jax.random.fold_in(own, axis_at), (parts,), jnp.float32, low / len(pieces), high / len(pieces)))
        factor_of = factor_of * jnp.repeat(steps, dims[axis_at] // parts).reshape([-1 if axis == axis_at else 1 for axis in range(len(dims))])
    return factor_of


def rank_bounds(number_of, skew):
    portions = [(1 << 20) // math.isqrt(grade ** skew) + 1 for grade in range(1, number_of + 1)]
    scale = 1 + sum(portions) // (1 << 30)
    return np.cumsum(np.array([max(1, weight // scale) for weight in portions]))


def ranked(key, extent, amount, lean):
    grid = rank_bounds(amount, lean)
    ticket = jax.random.randint(jax.random.fold_in(key, 1), extent, 0, int(grid[amount - 1]))
    standing = jnp.searchsorted(jnp.asarray(grid, jnp.int32), ticket, side="right")
    return jax.random.permutation(jax.random.fold_in(key, 2), amount)[standing].astype(jnp.int32)


def profile(count, total, bound, lean):
    portions = [(1 << 20) // math.isqrt(rank ** lean) + 1 for rank in range(2, count + 1)]
    spare, counts = total - bound - (count - 1), [1] * (count - 1)
    while spare > 0:
        movable = [i for i in range(count - 1) if counts[i] < bound]
        whole, remaining = sum([portions[i] for i in movable]), spare
        for i in movable:
            extra = min(bound - counts[i], max(1, remaining * portions[i] // whole), spare)
            counts[i] = counts[i] + extra
            spare = spare - extra
    return np.array([bound] + counts)


def ragged_sizes(own_key, count, total, reach, lean):
    if count == 2:
        one = jax.random.randint(own_key, (), max(1, total - reach), min(reach, total - 1) + 1)
        return jnp.stack([one, total - one])
    sizes = jnp.asarray(profile(count, total, reach, lean), jnp.int32)
    twos = (count - 1) // 2
    source_of, sink = sizes[1:1 + 2 * twos:2], sizes[2:2 + 2 * twos:2]
    slack = jnp.minimum(source_of - 1, reach - sink)
    shifted = jax.random.randint(jax.random.fold_in(own_key, 1), (twos,), 0, 1 << 20) % (slack + 1)
    sizes = sizes.at[1:1 + 2 * twos:2].set(source_of - shifted).at[2:2 + 2 * twos:2].set(sink + shifted)
    return sizes[jax.random.permutation(jax.random.fold_in(own_key, 2), count)]


def normal_values(stream_key, shape, deviation, limit, cuts=(), kind=jnp.bfloat16):
    result = deviation * jax.random.normal(stream_key, shape, jnp.float32)
    if cuts:
        result = result * levels(stream_key, shape, cuts, -0.22, 0.18)
    return jnp.clip(result, -limit, limit).astype(kind)


def setup_inputs(seed: int = 0) -> dict:
    arg_keys = jax.random.split(jax.random.key(seed), 10)
    features = normal_values(arg_keys[0], (NODES, WIDTH), 1.0, 6.0, ((0, 128),))
    weight = normal_values(arg_keys[1], (WIDTH, WIDTH), WIDTH ** -0.5, 0.375)
    adjacency = normal_values(arg_keys[2], (GRID_ROWS, GRID_COLS, SLOTS, BLOCK, BLOCK), (BLOCK * BLOCK * SLOTS // NODE_DEV) ** -0.5, 0.0546875, ((0, 8), (1, 16)))
    block_rows = set_ends(ranked(arg_keys[3], (GRID_ROWS, GRID_COLS, SLOTS), ROW_BLOCKS, 1), jax.random.fold_in(arg_keys[3], 3), 0, ROW_BLOCKS - 1).astype(jnp.int32)
    block_cols = set_ends(jax.random.randint(arg_keys[4], (GRID_ROWS, GRID_COLS, SLOTS), 0, COL_BLOCKS), jax.random.fold_in(arg_keys[4], 1), 0, COL_BLOCKS - 1).astype(jnp.int32)
    live_blocks = draw_live_blocks(jax.random.fold_in(arg_keys[9], 71), 0)
    part_gains = jnp.clip(jnp.exp(jax.random.uniform(arg_keys[6], (PARTS_SIZE, WIDTH), jnp.float32, math.log(0.5), math.log(2.0))), 0.5, 2.0)
    partition = jnp.searchsorted(jnp.cumsum(ragged_sizes(arg_keys[7], PARTS_SIZE, NODES, 4 * NODE_DEV, 1)), jnp.arange(NODES), side="right").astype(jnp.int32)
    cotangent = normal_values(arg_keys[8], (NODES, WIDTH), 1.0, 6.0, ((0, 128),))
    return {"features": features, "weight": weight, "adjacency": adjacency, "block_rows": block_rows, "block_cols": block_cols, "live_blocks": live_blocks, "part_gains": part_gains, "partition": partition, "cotangent": cotangent}


def silu_slope(values):
    sig = jax.nn.sigmoid(values)
    return sig * (1.0 + values * (1.0 - sig))

def rounded(values):
    return lax.optimization_barrier(values.astype(jnp.bfloat16)).astype(jnp.float32)

def tile_sum(tile_values, row_index, col_index, live_count, panels, out_blocks, forward):
    slot_mask = (jnp.arange(SLOTS, dtype=jnp.int32) < live_count).astype(jnp.float32)
    weights = tile_values.astype(jnp.float32) * slot_mask[:, None, None]
    panel_blocks = panels.astype(jnp.float32).reshape(-1, BLOCK, WIDTH)
    if forward:
        products = jnp.einsum('kab,kbf->kaf', weights, panel_blocks[col_index])
        targets = row_index
    else:
        products = jnp.einsum('kab,kaf->kbf', weights, panel_blocks[row_index])
        targets = col_index
    totals = jnp.zeros((out_blocks, BLOCK, WIDTH), jnp.float32).at[targets].add(products)
    return totals.reshape(out_blocks * BLOCK, WIDTH)

def reference(features, weight, adjacency, block_rows, block_cols, live_blocks, part_gains, partition, cotangent):
    hidden = jnp.dot(features, weight, preferred_element_type=jnp.float32).astype(jnp.bfloat16)
    hidden_grid = hidden.reshape(GRID_ROWS, GRID_COLS, NODE_DEV, WIDTH)

    def forward_tile(position, running):
        tile_row = position // GRID_COLS
        tile_col = position % GRID_COLS
        panels = hidden_grid[:, tile_col].reshape(GRID_ROWS * NODE_DEV, WIDTH)
        part_sum = tile_sum(adjacency[tile_row, tile_col], block_rows[tile_row, tile_col], block_cols[tile_row, tile_col], live_blocks[tile_row, tile_col], panels, ROW_BLOCKS, True)
        return running.at[tile_row].add(rounded(part_sum))
    row_sums = lax.fori_loop(0, GRID_ROWS * GRID_COLS, forward_tile, jnp.zeros((GRID_ROWS, GRID_COLS * NODE_DEV, WIDTH), jnp.float32))
    summed = row_sums.reshape(NODES, WIDTH)
    activated = jax.nn.silu(summed)
    row_gains = part_gains[partition]
    layer_out = (activated * row_gains).astype(jnp.bfloat16)
    agg_grad = (cotangent.astype(jnp.float32) * row_gains * silu_slope(summed)).astype(jnp.bfloat16)
    grad_grid = agg_grad.reshape(GRID_ROWS, GRID_COLS * NODE_DEV, WIDTH)

    def backward_tile(position, running):
        tile_row = position // GRID_COLS
        tile_col = position % GRID_COLS
        part_sum = tile_sum(adjacency[tile_row, tile_col], block_rows[tile_row, tile_col], block_cols[tile_row, tile_col], live_blocks[tile_row, tile_col], grad_grid[tile_row], COL_BLOCKS, False)
        return running.at[tile_col].add(rounded(part_sum))
    col_sums = lax.fori_loop(0, GRID_ROWS * GRID_COLS, backward_tile, jnp.zeros((GRID_COLS, GRID_ROWS * NODE_DEV, WIDTH), jnp.float32))
    hidden_grad = col_sums.reshape(GRID_COLS, GRID_ROWS, NODE_DEV, WIDTH).transpose(1, 0, 2, 3).reshape(NODES, WIDTH).astype(jnp.bfloat16)
    feature_grad = jnp.dot(hidden_grad, weight.T, preferred_element_type=jnp.float32).astype(jnp.bfloat16)
    weight_grad = jnp.dot(features.T, hidden_grad, preferred_element_type=jnp.float32) / jnp.sqrt(jnp.float32(NODES))
    part_sums = jax.ops.segment_sum(cotangent.astype(jnp.float32) * activated, partition, num_segments=PARTS_SIZE)
    sizes_part = jax.ops.segment_sum(jnp.ones((NODES,), jnp.float32), partition, num_segments=PARTS_SIZE)
    gain_grad = part_sums / jnp.sqrt(sizes_part)[:, None]
    return (layer_out, feature_grad, weight_grad, gain_grad)
```

```python
import jax
import jax.numpy as jnp
from jax import lax
from jax.experimental import pallas as pl
from jax.experimental.pallas import tpu as pltpu
from jax.sharding import PartitionSpec as P

BLOCK = 128
SLOTS = 384
WIDTH = 256
CHUNKS = 2
LANES = 128
PARTS = 64
NODES = 65536
UNROLL = 16
MESH = pl.DeviceIdType.MESH
F32 = jnp.float32
BF16 = jnp.bfloat16


def order_slots(target, other, live_count, count, order):
    slot = jnp.arange(SLOTS, dtype=jnp.int32)
    key = jnp.where(slot < live_count, target, count)
    mark = key * 512 + slot
    rank = jnp.sum((mark[None, :] < mark[:, None]).astype(jnp.int32), axis=1)
    packed = (slot * 128 + key) * 128 + other
    hit = rank[None, :] == slot[:, None]
    ranked = jnp.sum(jnp.where(hit, packed[None, :], 0), axis=1)
    sorted_key = (ranked // 128) % 128
    keep = jnp.concatenate([jnp.zeros((1,), F32), (sorted_key[1:] == sorted_key[:-1]).astype(F32)])
    upto = jnp.sum((key[None, :] <= order[:, None]).astype(jnp.int32), axis=1)
    some = jnp.any(key[None, :] == order[:, None], axis=1)
    last = jnp.where(some, upto - 1, SLOTS)
    return ranked // (128 * 128), ranked % 128, keep, last


def silu_parts(v):
    g = 1.0 / (1.0 + jnp.exp(-v))
    return v * g, g * (1.0 + v * (1.0 - g))


def kernel(
    perm_f, idx_f, keep_f, last_f, perm_b, idx_b, keep_b, last_b,
    x_ref, w_ref, a_hbm, pg_ref, part_ref, cot_ref,
    lo_ref, fg_ref, wg_ref, gg_ref,
    a_v, s_v, h0, h1, r0, r1, cx0, cx1, t0, t1, zr0, zr1, ux0, ux1, xr0, xr1,
    g0, g1, p0, p1, yr0, yr1, vx0, vx1, vr0, vr1,
    wp0, wp1, wr0, wr1, ws0, ws1, wc0, wc1, wf0, wf1,
    rg_v, mt_v, xt_v, hg_v,
    a_sem, send, recv,
):
    row = lax.axis_index("row")
    col = lax.axis_index("col")
    xl, y = row // 4, row % 4
    z, xh, core = col // 4, (col // 2) % 2, col % 2

    def at(xl=xl, y=y, z=z, xh=xh, core=core):
        return (xl * 4 + y, z * 4 + xh * 2 + core)

    H, R, CX, T, ZR = (h0, h1), (r0, r1), (cx0, cx1), (t0, t1), (zr0, zr1)
    UX, XR, G, PP, YR = (ux0, ux1), (xr0, xr1), (g0, g1), (p0, p1), (yr0, yr1)
    VX, VR = (vx0, vx1), (vr0, vr1)
    WP, WR, WS, WC, WF = (wp0, wp1), (wr0, wr1), (ws0, ws1), (wc0, wc1), (wf0, wf1)

    started = []

    def push(src, dst, device):
        n = len(started)
        copy = pltpu.make_async_remote_copy(
            src_ref=src, dst_ref=dst, send_sem=send.at[n], recv_sem=recv.at[n],
            device_id=device, device_id_type=MESH,
        )
        copy.start()
        started.append(copy)
        return copy

    pieces = 4
    step = SLOTS // pieces
    loads = [
        pltpu.make_async_copy(
            a_hbm.at[pl.ds(n * step, step)], a_v.at[pl.ds(n * step, step)], a_sem.at[n]
        )
        for n in range(pieces)
    ]
    for load in loads:
        load.start()

    barrier = pltpu.get_barrier_semaphore()
    for d in range(1, 8):
        pl.semaphore_signal(barrier, inc=1, device_id=((row + d) % 8, col), device_id_type=MESH)
    for d in range(1, 16):
        pl.semaphore_signal(barrier, inc=1, device_id=(row, (col + d) % 16), device_id_type=MESH)

    own_h = pl.ds(row * 4, 4)
    for c in range(CHUNKS):
        hidden = jnp.dot(x_ref[...], w_ref[:, c * LANES:(c + 1) * LANES], preferred_element_type=F32)
        H[c][own_h] = hidden.astype(BF16).reshape(4, BLOCK, LANES)
    pl.semaphore_wait(barrier, 22)

    ag_x, ag_y = {}, {}

    def gather_x(c):
        mine = H[c].at[own_h]
        ag_x[c] = push(mine, mine, at(xl=1 - xl))

    def gather_y_own(c):
        mine = H[c].at[own_h]
        ag_y[c] = [push(mine, mine, at(y=(y + d) % 4)) for d in (1, 3, 2)]

    def gather_y_other(c):
        ag_x[c].wait_recv()
        other = H[c].at[pl.ds(((1 - xl) * 4 + y) * 4, 4)]
        ag_y[c] += [push(other, other, at(y=(y + d) % 4)) for d in (1, 3, 2)]

    def tile_pass(c, forward, first, stop, acc):
        perm, idx, keep = (perm_f, idx_f, keep_f) if forward else (perm_b, idx_b, keep_b)

        def body(t, acc):
            for u in range(UNROLL):
                k = t * UNROLL + u
                block = a_v[perm[k]]
                panel = (H if forward else G)[c][idx[k]]
                if forward:
                    term = jnp.dot(block, panel, preferred_element_type=F32)
                else:
                    term = jnp.dot(panel, block, preferred_element_type=F32)
                acc = acc * keep[k] + term
                s_v[k] = acc.astype(BF16)
            return acc

        return lax.fori_loop(first // UNROLL, stop // UNROLL, body, acc)

    def collect(dst, last, count):
        def body(q, carry):
            for u in range(8):
                dst[q * 8 + u] = s_v[last[q * 8 + u]]
            return carry

        lax.fori_loop(0, count // 8, body, 0)

    zero = jnp.zeros((BLOCK, LANES), F32)

    def core_send(c):
        return push(R[c].at[pl.ds((1 - core) * 32, 32)], CX[c], at(core=1 - core))

    def core_add(c, copy):
        copy.wait_recv()

        def body(b, carry):
            T[c][b] = (R[c][core * 32 + b].astype(F32) + CX[c][b].astype(F32)).astype(BF16)
            return carry

        lax.fori_loop(0, 32, body, 0)

    def z_send(c):
        return [
            push(T[c].at[pl.ds(((z + d) % 4) * 8, 8)], ZR[c].at[d - 1], at(z=(z + d) % 4))
            for d in (1, 3, 2)
        ]

    def z_sum(c, which):
        rows = pl.ds(z * 8 + which * 4, 4)
        total = T[c][rows].astype(F32)
        for d in range(3):
            total = total + ZR[c][d, pl.ds(which * 4, 4)].astype(F32)
        return total

    def x_send(c, copies):
        for copy in copies:
            copy.wait_recv()
        UX[c][...] = z_sum(c, 1 - xh).astype(BF16)
        return push(UX[c], XR[c], at(xh=1 - xh))

    def slot_of(zz, xx, cc):
        return pl.ds(cc * 32 + (zz * 2 + xx) * 4, 4)

    def activate(c, copy):
        copy.wait_recv()
        lanes = slice(c * LANES, (c + 1) * LANES)
        summed = (z_sum(c, xh) + XR[c][...].astype(F32)).reshape(4 * BLOCK, LANES)
        act, slope = silu_parts(summed)
        gains = rg_v[:, lanes]
        cot = cot_ref[:, lanes].astype(F32)
        grad = cot * gains * slope
        for b in range(4):
            G[c][core * 32 + (z * 2 + xh) * 4 + b] = grad[b * BLOCK:(b + 1) * BLOCK].T.astype(BF16)
        return act, gains, cot

    def after_activate(c, held):
        act, gains, cot = held
        lanes = slice(c * LANES, (c + 1) * LANES)
        lo_ref[:, lanes] = (act * gains).astype(BF16)
        terms = jnp.dot(mt_v[...], cot * act, precision=lax.Precision.HIGHEST, preferred_element_type=F32)
        sizes = jnp.dot(
            mt_v[...], jnp.ones((4 * BLOCK, LANES), F32), preferred_element_type=F32
        )
        for i in range(8):
            WP[c][i, 32:40] = terms[i * 8:(i + 1) * 8]
            WP[c][i, 40:48] = sizes[i * 8:(i + 1) * 8]

    def grad_send(c):
        mine = G[c].at[slot_of(z, xh, core)]
        first = push(mine, mine, at(xh=1 - xh))
        zs = [push(mine, mine, at(z=(z + d) % 4)) for d in (1, 3, 2)]
        return first, zs, [push(mine, mine, at(core=1 - core))]

    def grad_forward(c, state):
        first, zs, cores = state
        first.wait_recv()
        other = G[c].at[slot_of(z, 1 - xh, core)]
        zs2 = [push(other, other, at(z=(z + d) % 4)) for d in (1, 3, 2)]
        cores.append(push(other, other, at(core=1 - core)))
        return zs, zs2, cores

    def grad_finish(c, state):
        zs, zs2, cores = state
        for xx, group in ((xh, zs), (1 - xh, zs2)):
            for d, copy in zip((1, 3, 2), group):
                copy.wait_recv()
                got = G[c].at[slot_of((z + 4 - d) % 4, xx, core)]
                cores.append(push(got, got, at(core=1 - core)))
        for copy in cores:
            copy.wait_recv()

    def y_send(c):
        return [
            push(PP[c].at[pl.ds(((y + d) % 4) * 8, 8)], YR[c].at[d - 1], at(y=(y + d) % 4))
            for d in (1, 3, 2)
        ]

    def y_sum(c, which):
        total = PP[c][pl.ds(y * 8 + which * 4, 4)].astype(F32)
        for d in range(3):
            total = total + YR[c][d, pl.ds(which * 4, 4)].astype(F32)
        return total

    def x2_send(c, copies):
        for copy in copies:
            copy.wait_recv()
        VX[c][...] = y_sum(c, 1 - xl).astype(BF16)
        return push(VX[c], VR[c], at(xl=1 - xl))

    def finish_hidden(c, copy):
        copy.wait_recv()
        lanes = slice(c * LANES, (c + 1) * LANES)
        total = y_sum(c, xl) + VR[c][...].astype(F32)
        for b in range(4):
            hg_v[b * BLOCK:(b + 1) * BLOCK, lanes] = total[b].T.astype(BF16)
        part = jnp.dot(xt_v[...], hg_v[:, lanes], preferred_element_type=F32)
        for i in range(8):
            WP[c][i, 0:32] = part[i * 32:(i + 1) * 32]
        return [
            push(WP[c].at[(row + d) % 8], WR[c].at[d - 1], ((row + d) % 8, col))
            for d in range(1, 8)
        ]

    def weight_cols(c, copies):
        total = WP[c][row]
        for d, copy in enumerate(copies):
            copy.wait_recv()
            total = total + WR[c][d]
        WS[c][...] = total
        return [
            push(WS[c], WC[c].at[d - 1], (row, (col + d) % 16)) for d in range(1, 16)
        ]

    def weight_rows(c, copies):
        total = jnp.zeros((48, LANES), F32)
        for copy in copies:
            copy.wait_recv()
        WC[c][15] = WS[c][...]
        for j in range(16):
            total = total + WC[c][(col + 15 - j) % 16]
        WF[c][row, 0:32] = total[0:32] / 256.0
        WF[c][row, 32:48] = total[32:48]
        mine = WF[c].at[row]
        return [push(mine, mine, ((row + d) % 8, col)) for d in range(1, 8)]

    def weight_out(c, copies):
        for copy in copies:
            copy.wait_recv()
        lanes = slice(c * LANES, (c + 1) * LANES)
        for i in range(8):
            wg_ref[i * 32:(i + 1) * 32, lanes] = WF[c][i, 0:32]
            gg_ref[i * 8:(i + 1) * 8, lanes] = WF[c][i, 32:40] / jnp.sqrt(WF[c][i, 40:48])

    gather_x(0)
    gather_y_own(0)
    gather_x(1)
    s_v[SLOTS] = jnp.zeros((BLOCK, LANES), BF16)
    gather_y_other(0)
    ids = lax.broadcasted_iota(jnp.int32, (PARTS, 4 * BLOCK), 0)
    mt_v[...] = (part_ref[...] == ids).astype(F32)
    rg_v[...] = lax.dot_general(
        mt_v[...], pg_ref[...], (((0,), (0,)), ((), ())),
        precision=lax.Precision.HIGHEST, preferred_element_type=F32,
    )
    xt_v[...] = x_ref[...].astype(F32).T.astype(BF16)
    for load in loads:
        load.wait()
    for copy in ag_y[0]:
        copy.wait_recv()
    gather_y_own(1)
    gather_y_other(1)

    tile_pass(0, True, 0, SLOTS, zero)
    collect(R[0], last_f, 64)
    cs0 = core_send(0)
    for copy in ag_y[1]:
        copy.wait_recv()
    acc = tile_pass(1, True, 0, 128, zero)
    core_add(0, cs0)
    zs0 = z_send(0)
    tile_pass(1, True, 128, SLOTS, acc)
    collect(R[1], last_f, 64)
    cs1 = core_send(1)
    xs0 = x_send(0, zs0)
    core_add(1, cs1)
    zs1 = z_send(1)
    held = activate(0, xs0)
    gs0 = grad_send(0)
    after_activate(0, held)
    gs0 = grad_forward(0, gs0)
    xs1 = x_send(1, zs1)
    held = activate(1, xs1)
    gs1 = grad_send(1)
    after_activate(1, held)
    gs1 = grad_forward(1, gs1)
    grad_finish(0, gs0)
    tile_pass(0, False, 0, SLOTS, zero)
    collect(PP[0], last_b, 32)
    ys0 = y_send(0)
    grad_finish(1, gs1)
    tile_pass(1, False, 0, SLOTS, zero)
    collect(PP[1], last_b, 32)
    vs0 = x2_send(0, ys0)
    ys1 = y_send(1)
    wr0_ = finish_hidden(0, vs0)
    wc0_ = weight_cols(0, wr0_)
    wf0_ = weight_rows(0, wc0_)
    vs1 = x2_send(1, ys1)
    wr1_ = finish_hidden(1, vs1)
    fg_ref[...] = lax.dot_general(
        hg_v[...], w_ref[...], (((1,), (1,)), ((), ())), preferred_element_type=F32
    ).astype(BF16)
    wc1_ = weight_cols(1, wr1_)
    weight_out(0, wf0_)
    wf1_ = weight_rows(1, wc1_)
    weight_out(1, wf1_)
    for copy in started:
        copy.wait_send()


def per_device(
    features, weight, adjacency, block_rows, block_cols, live_blocks, part_gains, partition, cotangent
):
    live = live_blocks[0, 0]
    rows, cols = block_rows[0, 0], block_cols[0, 0]
    place = jnp.arange(64, dtype=jnp.int32)
    row_order = ((place % 32) // 4 * 2 + place // 32) * 4 + place % 4
    spot = jnp.arange(32, dtype=jnp.int32)
    col_order = ((spot // 4 % 2) * 4 + spot // 8) * 4 + spot % 4
    row_place = (rows // 4 % 2) * 32 + (rows // 8) * 4 + rows % 4
    forward = order_slots(rows, cols, live, 64, row_order)
    backward = order_slots(cols, row_place, live, 32, col_order)

    nodes = features.shape[0]
    smem = pl.BlockSpec(memory_space=pltpu.SMEM)
    vmem = pl.BlockSpec(memory_space=pltpu.VMEM)
    hbm = pl.BlockSpec(memory_space=pl.ANY)

    def pair(shape, dtype=BF16):
        return [pltpu.VMEM(shape, dtype)] * 2

    tile = (BLOCK, LANES)
    copies = 2 * (1 + 3 + 3 + 1 + 3 + 1 + 5 + 4 + 6 + 3 + 1 + 7 + 15 + 7)
    outs = (
        jax.ShapeDtypeStruct((nodes, WIDTH), BF16),
        jax.ShapeDtypeStruct((nodes, WIDTH), BF16),
        jax.ShapeDtypeStruct((WIDTH, WIDTH), F32),
        jax.ShapeDtypeStruct((PARTS, WIDTH), F32),
    )
    return pl.pallas_call(
        kernel,
        out_shape=outs,
        in_specs=[smem] * 8 + [vmem, vmem, hbm, vmem, vmem, vmem],
        out_specs=(vmem,) * 4,
        scratch_shapes=[
            pltpu.VMEM((SLOTS,) + tile, BF16),
            pltpu.VMEM((SLOTS + 1,) + tile, BF16),
            *pair((32,) + tile), *pair((64,) + tile), *pair((32,) + tile), *pair((32,) + tile),
            *pair((3, 8) + tile), *pair((4,) + tile), *pair((4,) + tile),
            *pair((64,) + tile), *pair((32,) + tile), *pair((3, 8) + tile),
            *pair((4,) + tile), *pair((4,) + tile),
            *pair((8, 48, LANES), F32), *pair((7, 48, LANES), F32), *pair((48, LANES), F32),
            *pair((16, 48, LANES), F32), *pair((8, 48, LANES), F32),
            pltpu.VMEM((nodes, WIDTH), F32),
            pltpu.VMEM((PARTS, nodes), F32),
            pltpu.VMEM((WIDTH, nodes), BF16),
            pltpu.VMEM((nodes, WIDTH), BF16),
            pltpu.SemaphoreType.DMA((4,)),
            pltpu.SemaphoreType.DMA((copies,)),
            pltpu.SemaphoreType.DMA((copies,)),
        ],
        compiler_params=pltpu.CompilerParams(
            collective_id=0, has_side_effects=True, vmem_limit_bytes=60 * 2**20
        ),
    )(
        *forward, *backward,
        features, weight, adjacency[0, 0], part_gains, partition.reshape(1, nodes), cotangent,
    )


def solution(mesh):
    in_specs = (
        P(("row", "col"), None),
        P(),
        P("row", "col", None, None, None),
        P("row", "col", None),
        P("row", "col", None),
        P("row", "col"),
        P(),
        P(("row", "col")),
        P(("row", "col"), None),
    )
    out_specs = (P(("row", "col"), None), P(("row", "col"), None), P(), P())
    return jax.shard_map(
        per_device, mesh=mesh, in_specs=in_specs, out_specs=out_specs, check_vma=False
    )
```

```python
import jax
import jax.numpy as jnp
from jax import lax
from jax.experimental import pallas as pl
from jax.experimental.pallas import tpu as pltpu
from jax.sharding import PartitionSpec as P

BLOCK = 128
SLOTS = 384
WIDTH = 256
CHUNKS = 2
LANES = 128
PARTS = 64
NODES = 65536
UNROLL = 32
MESH = pl.DeviceIdType.MESH
F32 = jnp.float32
BF16 = jnp.bfloat16


def order_slots(target, other, live_count, count, order):
    slot = lax.broadcasted_iota(jnp.int32, (1, SLOTS), 1)

    def column(row):
        return jnp.broadcast_to(row, (LANES, SLOTS)).T

    def wide(tall):
        return jnp.concatenate([tall] * (SLOTS // LANES), axis=1)

    def total(flags):
        return jnp.sum(flags.astype(jnp.int32), axis=0, keepdims=True)

    key = jnp.where(slot < live_count, target, count)
    mark = key * 512 + slot
    key_col = column(key)
    mark_col = wide(column(mark))
    rank = total(mark_col < mark)
    below = total(mark_col < key * 512)
    keep = (rank != below).astype(jnp.int32)
    entry = wide(column((slot * 64 + other) * 2 + keep))
    hit = wide(column(rank)) == slot
    entries = jnp.sum(jnp.where(hit, entry, 0), axis=0, keepdims=True)
    upto = total(key_col <= order)
    some = total(key_col == order)
    return entries, jnp.where(some > 0, upto - 1, SLOTS)


def silu_parts(v):
    g = 1.0 / (1.0 + jnp.exp(-v))
    return v * g, g * (1.0 + v * (1.0 - g))


def kernel(
    rows_ref, cols_ref, live_ref, x_ref, w_ref, a_hbm, pg_ref, part_ref, cot_ref,
    lo_ref, fg_ref, wg_ref, gg_ref,
    table_v, table, a_v, s_v, h0, h1, r0, r1, cx0, cx1, t0, t1, g0, g1, p0, p1,
    ca0, ca1, cp0, cp1, cm0, cm1, cb0, cb1, cs0_, cs1_, cl0, cl1,
    ra0, ra1, rp0, rp1, rm0, rm1, rb0, rb1, rs0_, rs1_, rl0, rl1,
    wp0, wp1, wr0, wr1, ws0, ws1, wc0, wc1, wf0, wf1,
    rg_v, mt_v, xt_v, hg_v,
    a_sem, t_sem, send, recv,
):
    row = lax.axis_index("row")
    col = lax.axis_index("col")
    xl, y = row // 4, row % 4
    z, xh, core = col // 4, (col // 2) % 2, col % 2

    def at(xl=xl, y=y, z=z, xh=xh, core=core):
        return (xl * 4 + y, z * 4 + xh * 2 + core)

    H, R, CX, T, G, PP = (h0, h1), (r0, r1), (cx0, cx1), (t0, t1), (g0, g1), (p0, p1)
    COL = ((ca0, cp0, cm0, cb0, cs0_, cl0), (ca1, cp1, cm1, cb1, cs1_, cl1))
    ROW = ((ra0, rp0, rm0, rb0, rs0_, rl0), (ra1, rp1, rm1, rb1, rs1_, rl1))
    WP, WR, WS, WC, WF = (wp0, wp1), (wr0, wr1), (ws0, ws1), (wc0, wc1), (wf0, wf1)

    started = []

    def push(src, dst, device):
        n = len(started)
        copy = pltpu.make_async_remote_copy(
            src_ref=src, dst_ref=dst, send_sem=send.at[n], recv_sem=recv.at[n],
            device_id=device, device_id_type=MESH,
        )
        copy.start()
        started.append(copy)
        return copy

    def arrive(copies):
        for copy in copies:
            copy.wait_recv()

    pieces = 4
    step = SLOTS // pieces
    loads = [
        pltpu.make_async_copy(
            a_hbm.at[pl.ds(n * step, step)], a_v.at[pl.ds(n * step, step)], a_sem.at[n]
        )
        for n in range(pieces)
    ]

    barrier = pltpu.get_barrier_semaphore()
    for d in range(1, 8):
        pl.semaphore_signal(barrier, inc=1, device_id=((row + d) % 8, col), device_id_type=MESH)
    for d in range(1, 16):
        pl.semaphore_signal(barrier, inc=1, device_id=(row, (col + d) % 16), device_id_type=MESH)

    own_h = pl.ds(row * 4, 4)
    for c in range(CHUNKS):
        hidden = jnp.dot(x_ref[...], w_ref[:, c * LANES:(c + 1) * LANES], preferred_element_type=F32)
        H[c][own_h] = hidden.astype(BF16).reshape(4, BLOCK, LANES)
    pl.semaphore_wait(barrier, 22)

    row_ring, row_pair = (lambda d: at(y=(y + d) % 4)), at(xl=1 - xl)
    col_ring, col_pair = (lambda d: at(z=(z + d) % 4)), at(xh=1 - xh)
    hops = (1, 3, 2)

    def gather_pair(buf, slot_of, ring, pair, to_pair):
        mine = buf.at[pl.ds(slot_of(ring, pair), 4)]
        return push(mine, mine, to_pair)

    def gather_ring(buf, slot_of, ring, pair, to_ring):
        mine = buf.at[pl.ds(slot_of(ring, pair), 4)]
        return [push(mine, mine, to_ring(d)) for d in hops]

    def gather_on_pair(buf, slot_of, ring, pair, to_ring, pair_copy):
        pair_copy.wait_recv()
        other = buf.at[pl.ds(slot_of(ring, 1 - pair), 2)]
        return [push(other, other, to_ring(d)) for d in hops]

    def gather_on_ring(buf, slot_of, ring, pair, to_pair, ring_copies):
        out = []
        for d, copy in zip(hops, ring_copies):
            copy.wait_recv()
            got = buf.at[pl.ds(slot_of((ring + 4 - d) % 4, pair) + 2, 2)]
            out.append(push(got, got, to_pair))
        return out

    def row_slot(ring, pair):
        return (pair * 4 + ring) * 4

    def col_slot(ring, pair):
        return core * 32 + (ring * 2 + pair) * 4

    def sum_start(bufs, src, ring, pair, to_ring, to_pair):
        b_pair = push(src.at[pl.ds(16 + (1 - pair) * 8, 8)], bufs[1], to_pair)
        a_ring = [
            push(src.at[pl.ds(((ring + d) % 4) * 4, 4)], bufs[0].at[d - 1], to_ring(d)) for d in hops
        ]
        return b_pair, a_ring

    def sum_on_pair(bufs, src, ring, pair, to_ring, b_pair):
        b_pair.wait_recv()
        bufs[2][...] = (
            src[pl.ds(16 + pair * 8, 8)].astype(F32) + bufs[1][...].astype(F32)
        ).astype(BF16)
        return [
            push(bufs[2].at[pl.ds(((ring + d) % 4) * 2, 2)], bufs[3].at[d - 1], to_ring(d))
            for d in hops
        ]

    def first_half(bufs, src, ring, which):
        total = src[pl.ds(ring * 4 + which * 2, 2)].astype(F32)
        for d in range(3):
            total = total + bufs[0][d, pl.ds(which * 2, 2)].astype(F32)
        return total

    def sum_on_ring(bufs, src, ring, pair, to_pair, a_ring):
        arrive(a_ring)
        bufs[4][...] = first_half(bufs, src, ring, 1 - pair).astype(BF16)
        return push(bufs[4], bufs[5], to_pair)

    def sum_finish(bufs, src, ring, pair, b_ring, a_pair):
        arrive(b_ring)
        second = bufs[2][pl.ds(ring * 2, 2)].astype(F32)
        for d in range(3):
            second = second + bufs[3][d].astype(F32)
        a_pair.wait_recv()
        first = first_half(bufs, src, ring, pair) + bufs[5][...].astype(F32)
        return first[0], first[1], second[0], second[1]

    def tile_pass(c, forward, first, stop, acc):
        line = 0 if forward else 1
        panels = (H if forward else G)[c]

        def body(t, acc):
            for u in range(UNROLL):
                k = t * UNROLL + u
                entry = table[line, k]
                block = a_v[entry >> 7]
                panel = panels[(entry >> 1) & 63]
                if forward:
                    term = jnp.dot(block, panel, preferred_element_type=F32)
                else:
                    term = jnp.dot(panel, block, preferred_element_type=F32)
                acc = acc * (entry & 1).astype(F32) + term
                s_v[k] = acc.astype(BF16)
            return acc

        return lax.fori_loop(first // UNROLL, stop // UNROLL, body, acc)

    def collect(dst, line, count):
        def body(q, carry):
            for u in range(8):
                dst[q * 8 + u] = s_v[table[line, q * 8 + u]]
            return carry

        lax.fori_loop(0, count // 8, body, 0)

    zero = jnp.zeros((BLOCK, LANES), F32)

    def core_send(c):
        return push(R[c].at[pl.ds((1 - core) * 32, 32)], CX[c], at(core=1 - core))

    def core_add(c, copy):
        copy.wait_recv()

        def body(q, carry):
            for u in range(4):
                b = q * 4 + u
                T[c][b] = (R[c][core * 32 + b].astype(F32) + CX[c][b].astype(F32)).astype(BF16)
            return carry

        lax.fori_loop(0, 8, body, 0)

    def activate(c, blocks):
        lanes = slice(c * LANES, (c + 1) * LANES)
        held = []
        for b in range(4):
            nodes = slice(b * BLOCK, (b + 1) * BLOCK)
            act, slope = silu_parts(blocks[b])
            cot = cot_ref[nodes, lanes].astype(F32)
            grad = cot * rg_v[nodes, lanes] * slope
            G[c][col_slot(z, xh) + b] = grad.T.astype(BF16)
            held.append(act)
        return held

    def after_activate(c, held):
        lanes = slice(c * LANES, (c + 1) * LANES)
        act = jnp.concatenate(held, axis=0)
        lo_ref[:, lanes] = (act * rg_v[:, lanes]).astype(BF16)
        terms = jnp.dot(
            mt_v[...], cot_ref[:, lanes].astype(F32) * act,
            precision=lax.Precision.HIGHEST, preferred_element_type=F32,
        )
        for i in range(8):
            WP[c][i, 32:40] = terms[i * 8:(i + 1) * 8]

    to_core = at(core=1 - core)

    def share(c, ring, pair, first, count):
        got = G[c].at[pl.ds(col_slot(ring, pair) + first, count)]
        return push(got, got, to_core)

    def grad_send(c):
        pair_copy = gather_pair(G[c], col_slot, z, xh, col_pair)
        ring_copies = gather_ring(G[c], col_slot, z, xh, col_ring)
        return pair_copy, ring_copies, [share(c, z, xh, 0, 4)]

    def grad_on_pair(c, state):
        pair_copy, ring_copies, cores = state
        ring_a = gather_on_pair(G[c], col_slot, z, xh, col_ring, pair_copy)
        cores.append(share(c, z, 1 - xh, 0, 4))
        return ring_a, ring_copies, cores

    def grad_on_ring(c, state):
        ring_a, ring_copies, cores = state
        pair_b = gather_on_ring(G[c], col_slot, z, xh, col_pair, ring_copies)
        for d in hops:
            cores.append(share(c, (z + 4 - d) % 4, xh, 0, 4))
        return ring_a, pair_b, cores

    def grad_finish(c, state):
        ring_a, pair_b, cores = state
        for d, copy in zip(hops, ring_a):
            copy.wait_recv()
            cores.append(share(c, (z + 4 - d) % 4, 1 - xh, 0, 2))
        for d, copy in zip(hops, pair_b):
            copy.wait_recv()
            cores.append(share(c, (z + 4 - d) % 4, 1 - xh, 2, 2))
        arrive(cores)

    def finish_hidden(c, blocks):
        lanes = slice(c * LANES, (c + 1) * LANES)
        for b in range(4):
            hg_v[b * BLOCK:(b + 1) * BLOCK, lanes] = blocks[b].T.astype(BF16)
        part = jnp.dot(xt_v[...], hg_v[:, lanes], preferred_element_type=F32)
        for i in range(8):
            WP[c][i, 0:32] = part[i * 32:(i + 1) * 32]
        return [
            push(WP[c].at[(row + d) % 8], WR[c].at[d - 1], ((row + d) % 8, col))
            for d in range(1, 8)
        ]

    def weight_cols(c, copies):
        arrive(copies)
        total = WP[c][row]
        for d in range(7):
            total = total + WR[c][d]
        WS[c][...] = total
        return [
            push(WS[c], WC[c].at[d - 1], (row, (col + d) % 16)) for d in range(1, 16)
        ]

    def weight_rows(c, copies):
        arrive(copies)
        WC[c][15] = WS[c][...]
        total = jnp.zeros((48, LANES), F32)
        for j in range(16):
            total = total + WC[c][(col + 15 - j) % 16]
        WF[c][row, 0:32] = total[0:32] / 256.0
        WF[c][row, 32:48] = total[32:48]
        mine = WF[c].at[row]
        return [push(mine, mine, ((row + d) % 8, col)) for d in range(1, 8)]

    def weight_out(c, copies):
        arrive(copies)
        lanes = slice(c * LANES, (c + 1) * LANES)
        for i in range(8):
            wg_ref[i * 32:(i + 1) * 32, lanes] = WF[c][i, 0:32]
            gg_ref[i * 8:(i + 1) * 8, lanes] = WF[c][i, 32:40] / jnp.sqrt(WF[c][i, 40:48])

    gp0 = gather_pair(H[0], row_slot, y, xl, row_pair)
    gr0 = gather_ring(H[0], row_slot, y, xl, row_ring)
    for load in loads:
        load.start()
    gp1 = gather_pair(H[1], row_slot, y, xl, row_pair)
    spot = lax.broadcasted_iota(jnp.int32, (1, LANES), 1)
    rows, cols = rows_ref[...], cols_ref[...]
    block = rows % 4
    row_place = (rows // 4 % 2) * 32 + (rows // 8) * 4 + block
    within = spot % 32
    second = within - 16
    ring_at = jnp.where(within < 16, within // 4, second // 2 % 4)
    pair_at = jnp.where(within < 16, within // 2 % 2, second // 8)
    block_at = jnp.where(within < 16, within % 2, 2 + second % 2)
    row_order = ((ring_at * 2 + pair_at) * 2 + spot // 32) * 4 + block_at
    col_order = (pair_at * 4 + ring_at) * 4 + block_at
    live = live_ref[0, 0]
    entries, last = order_slots(rows, cols, live, 64, row_order)
    table_v[0:1] = entries
    table_v[2:3, 0:LANES] = last
    entries, last = order_slots(cols, row_place, live, 32, col_order)
    table_v[1:2] = entries
    table_v[3:4, 0:LANES] = last
    to_table = pltpu.make_async_copy(table_v, table, t_sem)
    to_table.start()
    ga0 = gather_on_pair(H[0], row_slot, y, xl, row_ring, gp0)
    s_v[SLOTS] = jnp.zeros((BLOCK, LANES), BF16)
    gb0 = gather_on_ring(H[0], row_slot, y, xl, row_pair, gr0)
    ids = lax.broadcasted_iota(jnp.int32, (PARTS, 4 * BLOCK), 0)
    mt_v[...] = (part_ref[...] == ids).astype(F32)
    sizes = jnp.dot(mt_v[...], jnp.ones((4 * BLOCK, LANES), F32), preferred_element_type=F32)
    for c in range(CHUNKS):
        for i in range(8):
            WP[c][i, 40:48] = sizes[i * 8:(i + 1) * 8]
    to_table.wait()
    for load in loads:
        load.wait()
    arrive(ga0 + gb0)
    gr1 = gather_ring(H[1], row_slot, y, xl, row_ring)
    ga1 = gather_on_pair(H[1], row_slot, y, xl, row_ring, gp1)

    acc = tile_pass(0, True, 0, 256, zero)
    gb1 = gather_on_ring(H[1], row_slot, y, xl, row_pair, gr1)
    tile_pass(0, True, 256, SLOTS, acc)
    collect(R[0], 2, 64)
    cs0 = core_send(0)
    rg_v[...] = lax.dot_general(
        mt_v[...], pg_ref[...], (((0,), (0,)), ((), ())),
        precision=lax.Precision.HIGHEST, preferred_element_type=F32,
    )
    xt_v[...] = x_ref[...].astype(F32).T.astype(BF16)
    arrive(ga1 + gb1)
    acc = tile_pass(1, True, 0, 64, zero)
    core_add(0, cs0)
    bp0, ar0 = sum_start(COL[0], T[0], z, xh, col_ring, col_pair)
    acc = tile_pass(1, True, 64, 288, acc)
    br0 = sum_on_pair(COL[0], T[0], z, xh, col_ring, bp0)
    tile_pass(1, True, 288, SLOTS, acc)
    collect(R[1], 2, 64)
    cs1 = core_send(1)
    ap0 = sum_on_ring(COL[0], T[0], z, xh, col_pair, ar0)
    core_add(1, cs1)
    held0 = activate(0, sum_finish(COL[0], T[0], z, xh, br0, ap0))
    gs0 = grad_send(0)
    bp1, ar1 = sum_start(COL[1], T[1], z, xh, col_ring, col_pair)
    after_activate(0, held0)
    gs0 = grad_on_pair(0, gs0)
    gs0 = grad_on_ring(0, gs0)
    br1 = sum_on_pair(COL[1], T[1], z, xh, col_ring, bp1)
    ap1 = sum_on_ring(COL[1], T[1], z, xh, col_pair, ar1)
    grad_finish(0, gs0)
    acc = tile_pass(0, False, 0, 64, zero)
    held1 = activate(1, sum_finish(COL[1], T[1], z, xh, br1, ap1))
    gs1 = grad_send(1)
    after_activate(1, held1)
    acc = tile_pass(0, False, 64, 192, acc)
    gs1 = grad_on_pair(1, gs1)
    acc = tile_pass(0, False, 192, 320, acc)
    gs1 = grad_on_ring(1, gs1)
    tile_pass(0, False, 320, SLOTS, acc)
    collect(PP[0], 3, 32)
    bq0, aq0 = sum_start(ROW[0], PP[0], y, xl, row_ring, row_pair)
    grad_finish(1, gs1)
    acc = tile_pass(1, False, 0, 256, zero)
    dq0 = sum_on_pair(ROW[0], PP[0], y, xl, row_ring, bq0)
    acc = tile_pass(1, False, 256, SLOTS, acc)
    collect(PP[1], 3, 32)
    bq1, aq1 = sum_start(ROW[1], PP[1], y, xl, row_ring, row_pair)
    eq0 = sum_on_ring(ROW[0], PP[0], y, xl, row_pair, aq0)
    wr0_ = finish_hidden(0, sum_finish(ROW[0], PP[0], y, xl, dq0, eq0))
    dq1 = sum_on_pair(ROW[1], PP[1], y, xl, row_ring, bq1)
    wc0_ = weight_cols(0, wr0_)
    eq1 = sum_on_ring(ROW[1], PP[1], y, xl, row_pair, aq1)
    wr1_ = finish_hidden(1, sum_finish(ROW[1], PP[1], y, xl, dq1, eq1))
    fg_ref[...] = lax.dot_general(
        hg_v[...], w_ref[...], (((1,), (1,)), ((), ())), preferred_element_type=F32
    ).astype(BF16)
    wf0_ = weight_rows(0, wc0_)
    wc1_ = weight_cols(1, wr1_)
    weight_out(0, wf0_)
    wf1_ = weight_rows(1, wc1_)
    weight_out(1, wf1_)
    for copy in started:
        copy.wait_send()


def hand_over(*refs):
    half = len(refs) // 2
    for src, dst in zip(refs[:half], refs[half:]):
        dst[...] = src[...]


def per_device(
    features, weight, adjacency, block_rows, block_cols, live_blocks, part_gains, partition, cotangent
):
    nodes = features.shape[0]
    smem = pl.BlockSpec(memory_space=pltpu.SMEM)
    vmem = pl.BlockSpec(memory_space=pltpu.VMEM)
    hbm = pl.BlockSpec(memory_space=pl.ANY)

    def pair(shape, dtype=BF16):
        return [pltpu.VMEM(shape, dtype)] * 2

    tile = (BLOCK, LANES)
    sums = [
        *pair((3, 4) + tile), *pair((8,) + tile), *pair((8,) + tile),
        *pair((3, 2) + tile), *pair((2,) + tile), *pair((2,) + tile),
    ]
    copies = 160
    outs = (
        jax.ShapeDtypeStruct((nodes, WIDTH), BF16),
        jax.ShapeDtypeStruct((nodes, WIDTH), BF16),
        jax.ShapeDtypeStruct((WIDTH, WIDTH), F32),
        jax.ShapeDtypeStruct((PARTS, WIDTH), F32),
    )
    results = pl.pallas_call(
        kernel,
        out_shape=outs,
        in_specs=[vmem, vmem, smem, vmem, vmem, hbm, vmem, vmem, vmem],
        out_specs=(vmem,) * 4,
        scratch_shapes=[
            pltpu.VMEM((8, SLOTS), jnp.int32),
            pltpu.SMEM((8, SLOTS), jnp.int32),
            pltpu.VMEM((SLOTS,) + tile, BF16),
            pltpu.VMEM((SLOTS + 1,) + tile, BF16),
            *pair((32,) + tile), *pair((64,) + tile), *pair((32,) + tile), *pair((32,) + tile),
            *pair((64,) + tile), *pair((32,) + tile),
            *sums, *sums,
            *pair((8, 48, LANES), F32), *pair((7, 48, LANES), F32), *pair((48, LANES), F32),
            *pair((16, 48, LANES), F32), *pair((8, 48, LANES), F32),
            pltpu.VMEM((nodes, WIDTH), F32),
            pltpu.VMEM((PARTS, nodes), F32),
            pltpu.VMEM((WIDTH, nodes), BF16),
            pltpu.VMEM((nodes, WIDTH), BF16),
            pltpu.SemaphoreType.DMA((4,)),
            pltpu.SemaphoreType.DMA,
            pltpu.SemaphoreType.DMA((copies,)),
            pltpu.SemaphoreType.DMA((copies,)),
        ],
        compiler_params=pltpu.CompilerParams(
            collective_id=0, has_side_effects=True, vmem_limit_bytes=60 * 2**20
        ),
    )(
        block_rows.reshape(1, SLOTS), block_cols.reshape(1, SLOTS), live_blocks,
        features, weight, adjacency[0, 0], part_gains, partition.reshape(1, nodes), cotangent,
    )
    return pl.pallas_call(
        hand_over,
        out_shape=outs,
        in_specs=[vmem] * 4,
        out_specs=(vmem,) * 4,
    )(*results)


def solution(mesh):
    in_specs = (
        P(("row", "col"), None),
        P(),
        P("row", "col", None, None, None),
        P("row", "col", None),
        P("row", "col", None),
        P("row", "col"),
        P(),
        P(("row", "col")),
        P(("row", "col"), None),
    )
    out_specs = (P(("row", "col"), None), P(("row", "col"), None), P(), P())
    return jax.shard_map(
        per_device, mesh=mesh, in_specs=in_specs, out_specs=out_specs, check_vma=False
    )
```

```python
import jax
import jax.numpy as jnp
from jax import lax
from jax.experimental import pallas as pl
from jax.experimental.pallas import tpu as pltpu
from jax.sharding import PartitionSpec as P

BLOCK = 128
SLOTS = 384
WIDTH = 256
CHUNKS = 2
LANES = 128
PARTS = 64
NODES = 65536
UNROLL = 32
MESH = pl.DeviceIdType.MESH
F32 = jnp.float32
BF16 = jnp.bfloat16


def order_slots(target, other, live_count, count, order):
    slot = lax.broadcasted_iota(jnp.int32, (1, SLOTS), 1)

    def column(row):
        return jnp.broadcast_to(row, (LANES, SLOTS)).T

    def wide(tall):
        return jnp.concatenate([tall] * (SLOTS // LANES), axis=1)

    def total(flags):
        return jnp.sum(flags.astype(jnp.int32), axis=0, keepdims=True)

    key = jnp.where(slot < live_count, target, count)
    mark = key * 512 + slot
    key_col = column(key)
    mark_col = wide(column(mark))
    rank = total(mark_col < mark)
    below = total(mark_col < key * 512)
    keep = (rank != below).astype(jnp.int32)
    entry = wide(column((slot * 64 + other) * 2 + keep))
    hit = wide(column(rank)) == slot
    entries = jnp.sum(jnp.where(hit, entry, 0), axis=0, keepdims=True)
    upto = total(key_col <= order)
    some = total(key_col == order)
    return entries, jnp.where(some > 0, upto - 1, SLOTS)


def silu_parts(v):
    g = 1.0 / (1.0 + jnp.exp(-v))
    return v * g, g * (1.0 + v * (1.0 - g))


def kernel(
    rows_ref, cols_ref, live_ref, x_ref, w_ref, a_hbm, pg_ref, part_ref, cot_ref,
    lo_ref, fg_ref, wg_ref, gg_ref,
    table_v, table, a_v, s_v, h0, h1, r0, r1, cx0, cx1, t0, t1, g0, g1, p0, p1,
    ca0, ca1, cp0, cp1, cm0, cm1, cb0, cb1, cs0_, cs1_, cl0, cl1,
    ra0, ra1, rp0, rp1, rm0, rm1, rb0, rb1, rs0_, rs1_, rl0, rl1,
    wp0, wp1, wr0, wr1, ws0, ws1, wc0, wc1, wf0, wf1,
    rg_v, mt_v, xg_v, hg_v,
    a_sem, t_sem, send, recv,
):
    row = lax.axis_index("row")
    col = lax.axis_index("col")
    xl, y = row // 4, row % 4
    z, xh, core = col // 4, (col // 2) % 2, col % 2

    def at(xl=xl, y=y, z=z, xh=xh, core=core):
        return (xl * 4 + y, z * 4 + xh * 2 + core)

    H, R, CX, T, G, PP = (h0, h1), (r0, r1), (cx0, cx1), (t0, t1), (g0, g1), (p0, p1)
    COL = ((ca0, cp0, cm0, cb0, cs0_, cl0), (ca1, cp1, cm1, cb1, cs1_, cl1))
    ROW = ((ra0, rp0, rm0, rb0, rs0_, rl0), (ra1, rp1, rm1, rb1, rs1_, rl1))
    WP, WR, WS, WC, WF = (wp0, wp1), (wr0, wr1), (ws0, ws1), (wc0, wc1), (wf0, wf1)

    started = []

    def push(src, dst, device):
        n = len(started)
        copy = pltpu.make_async_remote_copy(
            src_ref=src, dst_ref=dst, send_sem=send.at[n], recv_sem=recv.at[n],
            device_id=device, device_id_type=MESH,
        )
        copy.start()
        started.append(copy)
        return copy

    def arrive(copies):
        for copy in copies:
            copy.wait_recv()

    pieces = 4
    step = SLOTS // pieces
    loads = [
        pltpu.make_async_copy(
            a_hbm.at[pl.ds(n * step, step)], a_v.at[pl.ds(n * step, step)], a_sem.at[n]
        )
        for n in range(pieces)
    ]

    barrier = pltpu.get_barrier_semaphore()
    for d in range(1, 8):
        pl.semaphore_signal(barrier, inc=1, device_id=((row + d) % 8, col), device_id_type=MESH)
    for d in range(1, 16):
        pl.semaphore_signal(barrier, inc=1, device_id=(row, (col + d) % 16), device_id_type=MESH)

    for c in range(CHUNKS):
        hidden = jnp.dot(x_ref[...], w_ref[:, c * LANES:(c + 1) * LANES], preferred_element_type=F32)
        hidden = hidden.astype(BF16).reshape(4, BLOCK, LANES)
        H[c][pl.ds(y * 8 + xl * 2, 2)] = hidden[0:2]
        H[c][pl.ds(y * 8 + 4 + xl * 2, 2)] = hidden[2:4]
    pl.semaphore_wait(barrier, 22)

    row_ring, row_pair = (lambda d: at(y=(y + d) % 4)), at(xl=1 - xl)
    col_ring, col_pair = (lambda d: at(z=(z + d) % 4)), at(xh=1 - xh)
    hops = (1, 3, 2)

    def gather_start(buf, base, ring, pair, to_ring, to_pair):
        first = buf.at[pl.ds(base + ring * 8 + pair * 2, 2)]
        second = buf.at[pl.ds(base + ring * 8 + 4 + pair * 2, 2)]
        a_pair = push(first, first, to_pair)
        b_ring = [push(second, second, to_ring(d)) for d in hops]
        return a_pair, b_ring, push(second, second, to_pair)

    def gather_on_pair(buf, base, ring, to_ring, a_pair):
        a_pair.wait_recv()
        both = buf.at[pl.ds(base + ring * 8, 4)]
        return [push(both, both, to_ring(d)) for d in hops]

    def gather_on_ring(buf, base, ring, pair, to_pair, b_ring):
        out = []
        for d, copy in zip(hops, b_ring):
            copy.wait_recv()
            got = buf.at[pl.ds(base + (ring + 4 - d) % 4 * 8 + 4 + pair * 2, 2)]
            out.append(push(got, got, to_pair))
        return out

    def sum_start(bufs, src, ring, pair, to_ring, to_pair):
        b_pair = []
        for d in (2, 1, 3, 0):
            spot = (ring + d) % 4 * 2
            b_pair.append(
                push(src.at[pl.ds(16 + (1 - pair) * 8 + spot, 2)], bufs[1].at[pl.ds(spot, 2)], to_pair)
            )
        a_ring = [
            push(src.at[pl.ds(((ring + d) % 4) * 4, 4)], bufs[0].at[d - 1], to_ring(d)) for d in hops
        ]
        return b_pair, a_ring

    def sum_on_pair(bufs, src, ring, pair, to_ring, b_pair):
        out = []
        for d, copy in zip((2, 1, 3), b_pair):
            copy.wait_recv()
            spot = pl.ds((ring + d) % 4 * 2, 2)
            mine = src[pl.ds(16 + pair * 8 + (ring + d) % 4 * 2, 2)]
            bufs[2][spot] = (mine.astype(F32) + bufs[1][spot].astype(F32)).astype(BF16)
            out.append(push(bufs[2].at[spot], bufs[3].at[d - 1], to_ring(d)))
        return out, b_pair[3]

    def first_half(bufs, src, ring, which):
        total = src[pl.ds(ring * 4 + which * 2, 2)].astype(F32)
        for d in range(3):
            total = total + bufs[0][d, pl.ds(which * 2, 2)].astype(F32)
        return total

    def sum_on_ring(bufs, src, ring, pair, to_pair, a_ring):
        arrive(a_ring)
        bufs[4][...] = first_half(bufs, src, ring, 1 - pair).astype(BF16)
        return push(bufs[4], bufs[5], to_pair)

    def sum_finish(bufs, src, ring, pair, on_pair, a_pair):
        b_ring, b_own = on_pair
        b_own.wait_recv()
        arrive(b_ring)
        second = src[pl.ds(16 + pair * 8 + ring * 2, 2)].astype(F32)
        second = second + bufs[1][pl.ds(ring * 2, 2)].astype(F32)
        for d in range(3):
            second = second + bufs[3][d].astype(F32)
        a_pair.wait_recv()
        first = first_half(bufs, src, ring, pair) + bufs[5][...].astype(F32)
        return first[0], first[1], second[0], second[1]

    def tile_pass(c, forward, first, stop, acc):
        line = 0 if forward else 1
        panels = (H if forward else G)[c]

        def body(t, acc):
            for u in range(UNROLL):
                k = t * UNROLL + u
                entry = table[line, k]
                block = a_v[entry >> 7]
                panel = panels[(entry >> 1) & 63]
                if forward:
                    term = jnp.dot(block, panel, preferred_element_type=F32)
                else:
                    term = jnp.dot(panel, block, preferred_element_type=F32)
                acc = acc * (entry & 1).astype(F32) + term
                s_v[k] = acc.astype(BF16)
            return acc

        return lax.fori_loop(first // UNROLL, stop // UNROLL, body, acc)

    def collect(dst, line, count):
        def body(q, carry):
            for u in range(8):
                dst[q * 8 + u] = s_v[table[line, q * 8 + u]]
            return carry

        lax.fori_loop(0, count // 8, body, 0)

    zero = jnp.zeros((BLOCK, LANES), F32)

    def core_send(c):
        return push(R[c].at[pl.ds((1 - core) * 32, 32)], CX[c], at(core=1 - core))

    def core_add(c, copy):
        copy.wait_recv()

        def body(q, carry):
            for u in range(4):
                b = q * 4 + u
                T[c][b] = (R[c][core * 32 + b].astype(F32) + CX[c][b].astype(F32)).astype(BF16)
            return carry

        lax.fori_loop(0, 8, body, 0)

    def activate(c, blocks):
        lanes = slice(c * LANES, (c + 1) * LANES)
        held = []
        for b in range(4):
            nodes = slice(b * BLOCK, (b + 1) * BLOCK)
            act, slope = silu_parts(blocks[b])
            cot = cot_ref[nodes, lanes].astype(F32)
            grad = cot * rg_v[nodes, lanes] * slope
            G[c][core * 32 + z * 8 + b // 2 * 4 + xh * 2 + b % 2] = grad.T.astype(BF16)
            held.append(act)
        return held

    def after_activate(c, held):
        lanes = slice(c * LANES, (c + 1) * LANES)
        act = jnp.concatenate(held, axis=0)
        lo_ref[:, lanes] = (act * rg_v[:, lanes]).astype(BF16)
        terms = jnp.dot(
            mt_v[...], cot_ref[:, lanes].astype(F32) * act,
            precision=lax.Precision.HIGHEST, preferred_element_type=F32,
        )
        for i in range(8):
            WP[c][i, 32:40] = terms[i * 8:(i + 1) * 8]

    to_core = at(core=1 - core)

    def share(c, first, count):
        got = G[c].at[pl.ds(core * 32 + first, count)]
        return push(got, got, to_core)

    def grad_start(c):
        return gather_start(G[c], core * 32, z, xh, col_ring, col_pair)

    def grad_on_pair(c, state):
        a_pair, b_ring, b_pair = state
        return gather_on_pair(G[c], core * 32, z, col_ring, a_pair), b_ring, b_pair

    def grad_on_ring(c, state):
        a_ring, b_ring, b_pair = state
        b_other = gather_on_ring(G[c], core * 32, z, xh, col_pair, b_ring)
        b_pair.wait_recv()
        return a_ring, b_other, [share(c, z * 8, 8)]

    def grad_finish(c, state):
        a_ring, b_other, cores = state
        for half, copies in ((0, a_ring), (4, b_other)):
            for d, copy in zip(hops, copies):
                copy.wait_recv()
                cores.append(share(c, (z + 4 - d) % 4 * 8 + half, 4))
        arrive(cores)

    def finish_hidden(c, blocks):
        lanes = slice(c * LANES, (c + 1) * LANES)
        for b in range(4):
            hg_v[b * BLOCK:(b + 1) * BLOCK, lanes] = blocks[b].T.astype(BF16)

    def weight_part(c):
        part = jnp.zeros((LANES, WIDTH), F32)
        for i in range(8):
            for b in range(4):
                pair, ring = i // 4, i % 4
                spot = ring * 4 + pair * 2 + b if b < 2 else 16 + pair * 8 + ring * 2 + b - 2
                nodes = slice((i * 4 + b) * BLOCK, (i * 4 + b + 1) * BLOCK)
                part = part + jnp.dot(PP[c][spot], xg_v[nodes], preferred_element_type=F32)
        part = part.T
        for i in range(8):
            WP[c][i, 0:32] = part[i * 32:(i + 1) * 32]
        return [
            push(WP[c].at[(row + d) % 8], WR[c].at[d - 1], ((row + d) % 8, col))
            for d in range(1, 8)
        ]

    def weight_cols(c, copies):
        arrive(copies)
        total = WP[c][row]
        for d in range(7):
            total = total + WR[c][d]
        WS[c][...] = total
        return [
            push(WS[c], WC[c].at[d - 1], (row, (col + d) % 16)) for d in range(1, 16)
        ]

    def weight_rows(c, copies):
        arrive(copies)
        WC[c][15] = WS[c][...]
        total = jnp.zeros((48, LANES), F32)
        for j in range(16):
            total = total + WC[c][(col + 15 - j) % 16]
        WF[c][row, 0:32] = total[0:32] / 256.0
        WF[c][row, 32:48] = total[32:48]
        mine = WF[c].at[row]
        return [push(mine, mine, ((row + d) % 8, col)) for d in range(1, 8)]

    def weight_out(c, copies):
        arrive(copies)
        lanes = slice(c * LANES, (c + 1) * LANES)
        for i in range(8):
            wg_ref[i * 32:(i + 1) * 32, lanes] = WF[c][i, 0:32]
            gg_ref[i * 8:(i + 1) * 8, lanes] = WF[c][i, 32:40] / jnp.sqrt(WF[c][i, 40:48])

    gs0 = gather_start(H[0], 0, y, xl, row_ring, row_pair)
    for load in loads:
        load.start()
    spot = lax.broadcasted_iota(jnp.int32, (1, LANES), 1)
    rows, cols = rows_ref[...], cols_ref[...]
    block = rows % 4
    row_place = (
        rows // 4 % 2 * 32 + rows // 16 * 8 + block // 2 * 4 + rows // 8 % 2 * 2 + block % 2
    )
    block = cols % 4
    col_place = cols // 4 % 4 * 8 + block // 2 * 4 + cols // 16 * 2 + block % 2
    within = spot % 32
    second = within - 16
    ring_at = jnp.where(within < 16, within // 4, second // 2 % 4)
    pair_at = jnp.where(within < 16, within // 2 % 2, second // 8)
    block_at = jnp.where(within < 16, within % 2, 2 + second % 2)
    row_order = ((ring_at * 2 + pair_at) * 2 + spot // 32) * 4 + block_at
    col_order = (pair_at * 4 + ring_at) * 4 + block_at
    live = live_ref[0, 0]
    entries, last = order_slots(rows, col_place, live, 64, row_order)
    table_v[0:1] = entries
    table_v[2:3, 0:LANES] = last
    entries, last = order_slots(cols, row_place, live, 32, col_order)
    table_v[1:2] = entries
    table_v[3:4, 0:LANES] = last
    to_table = pltpu.make_async_copy(table_v, table, t_sem)
    to_table.start()
    ga0 = gather_on_pair(H[0], 0, y, row_ring, gs0[0])
    ids = lax.broadcasted_iota(jnp.int32, (PARTS, 4 * BLOCK), 0)
    mt_v[...] = (part_ref[...] == ids).astype(F32)
    xg_v[pl.ds(row * 512, 512)] = x_ref[...]
    s_v[SLOTS] = jnp.zeros((BLOCK, LANES), BF16)
    gb0 = gather_on_ring(H[0], 0, y, xl, row_pair, gs0[1])
    to_table.wait()
    for load in loads:
        load.wait()
    arrive(ga0 + gb0 + [gs0[2]])
    gs1 = gather_start(H[1], 0, y, xl, row_ring, row_pair)

    acc = tile_pass(0, True, 0, 160, zero)
    ga1 = gather_on_pair(H[1], 0, y, row_ring, gs1[0])
    acc = tile_pass(0, True, 160, 256, acc)
    gb1 = gather_on_ring(H[1], 0, y, xl, row_pair, gs1[1])
    tile_pass(0, True, 256, SLOTS, acc)
    collect(R[0], 2, 64)
    cs0 = core_send(0)
    sizes = jnp.dot(mt_v[...], jnp.ones((4 * BLOCK, LANES), F32), preferred_element_type=F32)
    for c in range(CHUNKS):
        for i in range(8):
            WP[c][i, 40:48] = sizes[i * 8:(i + 1) * 8]
    rg_v[...] = lax.dot_general(
        mt_v[...], pg_ref[...], (((0,), (0,)), ((), ())),
        precision=lax.Precision.HIGHEST, preferred_element_type=F32,
    )
    core_add(0, cs0)
    bp0, ar0 = sum_start(COL[0], T[0], z, xh, col_ring, col_pair)
    arrive(ga1 + gb1 + [gs1[2]])
    own_x = xg_v.at[pl.ds(row * 512, 512)]
    px = push(own_x, own_x, row_pair)
    rx = [push(own_x, own_x, row_ring(d)) for d in hops]
    acc = tile_pass(1, True, 0, 128, zero)
    br0 = sum_on_pair(COL[0], T[0], z, xh, col_ring, bp0)
    tile_pass(1, True, 128, SLOTS, acc)
    collect(R[1], 2, 64)
    cs1 = core_send(1)
    ap0 = sum_on_ring(COL[0], T[0], z, xh, col_pair, ar0)
    core_add(1, cs1)
    bp1, ar1 = sum_start(COL[1], T[1], z, xh, col_ring, col_pair)
    held0 = activate(0, sum_finish(COL[0], T[0], z, xh, br0, ap0))
    gg0 = grad_start(0)
    px.wait_recv()
    other_x = xg_v.at[pl.ds(((1 - xl) * 4 + y) * 512, 512)]
    rx += [push(other_x, other_x, row_ring(d)) for d in hops]
    br1 = sum_on_pair(COL[1], T[1], z, xh, col_ring, bp1)
    gg0 = grad_on_pair(0, gg0)
    after_activate(0, held0)
    gg0 = grad_on_ring(0, gg0)
    ap1 = sum_on_ring(COL[1], T[1], z, xh, col_pair, ar1)
    held1 = activate(1, sum_finish(COL[1], T[1], z, xh, br1, ap1))
    gg1 = grad_start(1)
    grad_finish(0, gg0)
    gg1 = grad_on_pair(1, gg1)
    acc = tile_pass(0, False, 0, 96, zero)
    gg1 = grad_on_ring(1, gg1)
    tile_pass(0, False, 96, SLOTS, acc)
    collect(PP[0], 3, 32)
    bq0, aq0 = sum_start(ROW[0], PP[0], y, xl, row_ring, row_pair)
    after_activate(1, held1)
    arrive(rx)
    grad_finish(1, gg1)
    acc = tile_pass(1, False, 0, 128, zero)
    dq0 = sum_on_pair(ROW[0], PP[0], y, xl, row_ring, bq0)
    acc = tile_pass(1, False, 128, SLOTS, acc)
    collect(PP[1], 3, 32)
    bq1, aq1 = sum_start(ROW[1], PP[1], y, xl, row_ring, row_pair)
    eq0 = sum_on_ring(ROW[0], PP[0], y, xl, row_pair, aq0)
    wr0_ = weight_part(0)
    wr1_ = weight_part(1)
    finish_hidden(0, sum_finish(ROW[0], PP[0], y, xl, dq0, eq0))
    dq1 = sum_on_pair(ROW[1], PP[1], y, xl, row_ring, bq1)
    wc0_ = weight_cols(0, wr0_)
    wc1_ = weight_cols(1, wr1_)
    eq1 = sum_on_ring(ROW[1], PP[1], y, xl, row_pair, aq1)
    wf0_ = weight_rows(0, wc0_)
    wf1_ = weight_rows(1, wc1_)
    finish_hidden(1, sum_finish(ROW[1], PP[1], y, xl, dq1, eq1))
    fg_ref[...] = lax.dot_general(
        hg_v[...], w_ref[...], (((1,), (1,)), ((), ())), preferred_element_type=F32
    ).astype(BF16)
    weight_out(0, wf0_)
    weight_out(1, wf1_)
    for copy in started:
        copy.wait_send()


def hand_over(*refs):
    half = len(refs) // 2
    for src, dst in zip(refs[:half], refs[half:]):
        dst[...] = src[...]


def per_device(
    features, weight, adjacency, block_rows, block_cols, live_blocks, part_gains, partition, cotangent
):
    nodes = features.shape[0]
    smem = pl.BlockSpec(memory_space=pltpu.SMEM)
    vmem = pl.BlockSpec(memory_space=pltpu.VMEM)
    hbm = pl.BlockSpec(memory_space=pl.ANY)

    def pair(shape, dtype=BF16):
        return [pltpu.VMEM(shape, dtype)] * 2

    tile = (BLOCK, LANES)
    sums = [
        *pair((3, 4) + tile), *pair((8,) + tile), *pair((8,) + tile),
        *pair((3, 2) + tile), *pair((2,) + tile), *pair((2,) + tile),
    ]
    copies = 176
    outs = (
        jax.ShapeDtypeStruct((nodes, WIDTH), BF16),
        jax.ShapeDtypeStruct((nodes, WIDTH), BF16),
        jax.ShapeDtypeStruct((WIDTH, WIDTH), F32),
        jax.ShapeDtypeStruct((PARTS, WIDTH), F32),
    )
    results = pl.pallas_call(
        kernel,
        out_shape=outs,
        in_specs=[vmem, vmem, smem, vmem, vmem, hbm, vmem, vmem, vmem],
        out_specs=(vmem,) * 4,
        scratch_shapes=[
            pltpu.VMEM((8, SLOTS), jnp.int32),
            pltpu.SMEM((8, SLOTS), jnp.int32),
            pltpu.VMEM((SLOTS,) + tile, BF16),
            pltpu.VMEM((SLOTS + 1,) + tile, BF16),
            *pair((32,) + tile), *pair((64,) + tile), *pair((32,) + tile), *pair((32,) + tile),
            *pair((64,) + tile), *pair((32,) + tile),
            *sums, *sums,
            *pair((8, 48, LANES), F32), *pair((7, 48, LANES), F32), *pair((48, LANES), F32),
            *pair((16, 48, LANES), F32), *pair((8, 48, LANES), F32),
            pltpu.VMEM((nodes, WIDTH), F32),
            pltpu.VMEM((PARTS, nodes), F32),
            pltpu.VMEM((8 * nodes, WIDTH), BF16),
            pltpu.VMEM((nodes, WIDTH), BF16),
            pltpu.SemaphoreType.DMA((4,)),
            pltpu.SemaphoreType.DMA,
            pltpu.SemaphoreType.DMA((copies,)),
            pltpu.SemaphoreType.DMA((copies,)),
        ],
        compiler_params=pltpu.CompilerParams(
            collective_id=0, has_side_effects=True, vmem_limit_bytes=60 * 2**20
        ),
    )(
        block_rows.reshape(1, SLOTS), block_cols.reshape(1, SLOTS), live_blocks,
        features, weight, adjacency[0, 0], part_gains, partition.reshape(1, nodes), cotangent,
    )
    return pl.pallas_call(
        hand_over,
        out_shape=outs,
        in_specs=[vmem] * 4,
        out_specs=(vmem,) * 4,
    )(*results)


def solution(mesh):
    in_specs = (
        P(("row", "col"), None),
        P(),
        P("row", "col", None, None, None),
        P("row", "col", None),
        P("row", "col", None),
        P("row", "col"),
        P(),
        P(("row", "col")),
        P(("row", "col"), None),
    )
    out_specs = (P(("row", "col"), None), P(("row", "col"), None), P(), P())
    return jax.shard_map(
        per_device, mesh=mesh, in_specs=in_specs, out_specs=out_specs, check_vma=False
    )
```

```python
import jax
import jax.numpy as jnp
from jax import lax
from jax.experimental import pallas as pl
from jax.experimental.pallas import tpu as pltpu
from jax.sharding import PartitionSpec as P

BLOCK = 128
SLOTS = 384
WIDTH = 256
CHUNKS = 2
LANES = 128
PARTS = 64
NODES = 65536
UNROLL = 32
MESH = pl.DeviceIdType.MESH
F32 = jnp.float32
BF16 = jnp.bfloat16


def order_slots(target, other, live_count, count, order):
    slot = lax.broadcasted_iota(jnp.int32, (1, SLOTS), 1)

    def column(row):
        return jnp.broadcast_to(row, (LANES, SLOTS)).T

    def wide(tall):
        return jnp.concatenate([tall] * (SLOTS // LANES), axis=1)

    def total(flags):
        return jnp.sum(flags.astype(jnp.int32), axis=0, keepdims=True)

    key = jnp.where(slot < live_count, target, count)
    mark = key * 512 + slot
    key_col = column(key)
    mark_col = wide(column(mark))
    rank = total(mark_col < mark)
    below = total(mark_col < key * 512)
    keep = (rank != below).astype(jnp.int32)
    entry = wide(column((slot * 64 + other) * 2 + keep))
    hit = wide(column(rank)) == slot
    entries = jnp.sum(jnp.where(hit, entry, 0), axis=0, keepdims=True)
    upto = total(key_col <= order)
    some = total(key_col == order)
    return entries, jnp.where(some > 0, upto - 1, SLOTS)


def silu_parts(v):
    g = 1.0 / (1.0 + jnp.exp(-v))
    return v * g, g * (1.0 + v * (1.0 - g))


def kernel(
    rows_ref, cols_ref, live_ref, x_ref, w_ref, a_hbm, pg_ref, part_ref, cot_ref,
    lo_ref, fg_ref, wg_ref, gg_ref,
    table_v, table, a_v, s_v, h0, h1, r0, r1, cx0, cx1, t0, t1, g0, g1, p0, p1,
    ca0, ca1, cp0, cp1, cm0, cm1, cb0, cb1, cs0_, cs1_, cl0, cl1,
    ra0, ra1, rp0, rp1, rm0, rm1, rb0, rb1, rs0_, rs1_, rl0, rl1,
    wp, wr, ws, wk, wc, wf,
    rg_v, mt_v, xg_v, hg_v,
    a_sem, t_sem, send, recv,
):
    row = lax.axis_index("row")
    col = lax.axis_index("col")
    xl, y = row // 4, row % 4
    z, xh, core = col // 4, (col // 2) % 2, col % 2

    def at(xl=xl, y=y, z=z, xh=xh, core=core):
        return (xl * 4 + y, z * 4 + xh * 2 + core)

    H, R, CX, T, G, PP = (h0, h1), (r0, r1), (cx0, cx1), (t0, t1), (g0, g1), (p0, p1)
    COL = ((ca0, cp0, cm0, cb0, cs0_, cl0), (ca1, cp1, cm1, cb1, cs1_, cl1))
    ROW = ((ra0, rp0, rm0, rb0, rs0_, rl0), (ra1, rp1, rm1, rb1, rs1_, rl1))

    started = []

    def push(src, dst, device):
        n = len(started)
        copy = pltpu.make_async_remote_copy(
            src_ref=src, dst_ref=dst, send_sem=send.at[n], recv_sem=recv.at[n],
            device_id=device, device_id_type=MESH,
        )
        copy.start()
        started.append(copy)
        return copy

    def arrive(copies):
        for copy in copies:
            copy.wait_recv()

    pieces = 4
    step = SLOTS // pieces
    loads = [
        pltpu.make_async_copy(
            a_hbm.at[pl.ds(n * step, step)], a_v.at[pl.ds(n * step, step)], a_sem.at[n]
        )
        for n in range(pieces)
    ]

    barrier = pltpu.get_barrier_semaphore()
    near = [at(xl=1 - xl), at(xh=1 - xh), at(core=1 - core)]
    near += [at(y=(y + d) % 4) for d in (1, 3, 2)] + [at(z=(z + d) % 4) for d in (1, 3, 2)]
    for device in near:
        pl.semaphore_signal(barrier, inc=1, device_id=device, device_id_type=MESH)

    for c in range(CHUNKS):
        hidden = jnp.dot(x_ref[...], w_ref[:, c * LANES:(c + 1) * LANES], preferred_element_type=F32)
        hidden = hidden.astype(BF16).reshape(4, BLOCK, LANES)
        H[c][pl.ds(y * 8 + xl * 2, 2)] = hidden[0:2]
        H[c][pl.ds(y * 8 + 4 + xl * 2, 2)] = hidden[2:4]
    pl.semaphore_wait(barrier, 9)

    row_ring, row_pair = (lambda d: at(y=(y + d) % 4)), at(xl=1 - xl)
    col_ring, col_pair = (lambda d: at(z=(z + d) % 4)), at(xh=1 - xh)
    hops = (1, 3, 2)

    def gather_start(buf, base, ring, pair, to_ring, to_pair):
        first = buf.at[pl.ds(base + ring * 8 + pair * 2, 2)]
        second = buf.at[pl.ds(base + ring * 8 + 4 + pair * 2, 2)]
        a_pair = push(first, first, to_pair)
        b_ring = [push(second, second, to_ring(d)) for d in hops]
        return a_pair, b_ring, push(second, second, to_pair)

    def gather_on_pair(buf, base, ring, to_ring, a_pair):
        a_pair.wait_recv()
        both = buf.at[pl.ds(base + ring * 8, 4)]
        return [push(both, both, to_ring(d)) for d in hops]

    def gather_on_ring(buf, base, ring, pair, to_pair, b_ring):
        out = []
        for d, copy in zip(hops, b_ring):
            copy.wait_recv()
            got = buf.at[pl.ds(base + (ring + 4 - d) % 4 * 8 + 4 + pair * 2, 2)]
            out.append(push(got, got, to_pair))
        return out

    def gather_second(buf, base, ring, pair, to_ring, b_pair):
        b_pair.wait_recv()
        other = buf.at[pl.ds(base + ring * 8 + 4 + (1 - pair) * 2, 2)]
        return [push(other, other, to_ring(d)) for d in hops]

    def sum_start_pair(bufs, src, ring, pair, to_pair):
        b_pair = []
        for d in (2, 1, 3, 0):
            spot = (ring + d) % 4 * 2
            b_pair.append(
                push(src.at[pl.ds(16 + (1 - pair) * 8 + spot, 2)], bufs[1].at[pl.ds(spot, 2)], to_pair)
            )
        return b_pair

    def sum_start_ring(bufs, src, ring, to_ring):
        return [
            push(src.at[pl.ds(((ring + d) % 4) * 4, 4)], bufs[0].at[d - 1], to_ring(d)) for d in hops
        ]

    def row_start(c):
        b_pair = sum_start_pair(ROW[c], PP[c], y, xl, row_pair)
        return b_pair, sum_start_ring(ROW[c], PP[c], y, row_ring)

    def sum_on_pair(bufs, src, ring, pair, to_ring, b_pair):
        out = []
        for d, copy in zip((2, 1, 3), b_pair):
            copy.wait_recv()
            spot = pl.ds((ring + d) % 4 * 2, 2)
            mine = src[pl.ds(16 + pair * 8 + (ring + d) % 4 * 2, 2)]
            bufs[2][spot] = (mine.astype(F32) + bufs[1][spot].astype(F32)).astype(BF16)
            out.append(push(bufs[2].at[spot], bufs[3].at[d - 1], to_ring(d)))
        return out, b_pair[3]

    def first_half(bufs, src, ring, which):
        total = src[pl.ds(ring * 4 + which * 2, 2)].astype(F32)
        for d in range(3):
            total = total + bufs[0][d, pl.ds(which * 2, 2)].astype(F32)
        return total

    def sum_on_ring(bufs, src, ring, pair, to_pair, a_ring):
        arrive(a_ring)
        bufs[4][...] = first_half(bufs, src, ring, 1 - pair).astype(BF16)
        return push(bufs[4], bufs[5], to_pair)

    def sum_finish(bufs, src, ring, pair, on_pair, a_pair):
        b_ring, b_own = on_pair
        b_own.wait_recv()
        arrive(b_ring)
        second = src[pl.ds(16 + pair * 8 + ring * 2, 2)].astype(F32)
        second = second + bufs[1][pl.ds(ring * 2, 2)].astype(F32)
        for d in range(3):
            second = second + bufs[3][d].astype(F32)
        a_pair.wait_recv()
        first = first_half(bufs, src, ring, pair) + bufs[5][...].astype(F32)
        return first[0], first[1], second[0], second[1]

    def tile_pass(c, forward, first, stop, acc):
        line = 0 if forward else 1
        panels = (H if forward else G)[c]

        def body(t, acc):
            for u in range(UNROLL):
                k = t * UNROLL + u
                entry = table[line, k]
                block = a_v[entry >> 7]
                panel = panels[(entry >> 1) & 63]
                if forward:
                    term = jnp.dot(block, panel, preferred_element_type=F32)
                else:
                    term = jnp.dot(panel, block, preferred_element_type=F32)
                acc = acc * (entry & 1).astype(F32) + term
                s_v[k] = acc.astype(BF16)
            return acc

        return lax.fori_loop(first // UNROLL, stop // UNROLL, body, acc)

    def collect(dst, line, first):
        def body(q, carry):
            for u in range(8):
                b = first + q * 8 + u
                dst[b] = s_v[table[line, b]]
            return carry

        lax.fori_loop(0, 4, body, 0)

    zero = jnp.zeros((BLOCK, LANES), F32)

    core_order = (16 + (1 - xh) * 8, 0, 8, 16 + xh * 8)

    def core_send(c):
        return [
            push(R[c].at[pl.ds((1 - core) * 32 + n, 8)], CX[c].at[pl.ds(n, 8)], at(core=1 - core))
            for n in core_order
        ]

    def core_add(c, copies, parts):
        for p in parts:
            copies[p].wait_recv()
            for u in range(8):
                b = core_order[p] + u
                T[c][b] = (R[c][core * 32 + b].astype(F32) + CX[c][b].astype(F32)).astype(BF16)

    def core_start(c, copies):
        core_add(c, copies, (0,))
        b_pair = sum_start_pair(COL[c], T[c], z, xh, col_pair)
        core_add(c, copies, (1, 2))
        a_ring = sum_start_ring(COL[c], T[c], z, col_ring)
        core_add(c, copies, (3,))
        return b_pair, a_ring

    def activate(c, blocks):
        lanes = slice(c * LANES, (c + 1) * LANES)
        held = []
        for b in range(4):
            nodes = slice(b * BLOCK, (b + 1) * BLOCK)
            act, slope = silu_parts(blocks[b])
            cot = cot_ref[nodes, lanes].astype(F32)
            grad = cot * rg_v[nodes, lanes] * slope
            G[c][core * 32 + z * 8 + b // 2 * 4 + xh * 2 + b % 2] = grad.T.astype(BF16)
            held.append(act)
        return held

    def after_activate(c, held):
        lanes = slice(c * LANES, (c + 1) * LANES)
        act = jnp.concatenate(held, axis=0)
        lo_ref[:, lanes] = (act * rg_v[:, lanes]).astype(BF16)
        terms = jnp.dot(
            mt_v[...], cot_ref[:, lanes].astype(F32) * act,
            precision=lax.Precision.HIGHEST, preferred_element_type=F32,
        )
        for i in range(8):
            wp[i, c * 48 + 32:c * 48 + 40] = terms[i * 8:(i + 1) * 8]

    to_core = at(core=1 - core)

    def share(c, first, count):
        got = G[c].at[pl.ds(core * 32 + first, count)]
        return push(got, got, to_core)

    def grad_start(c):
        return gather_start(G[c], core * 32, z, xh, col_ring, col_pair)

    def grad_on_pair(c, state):
        a_pair, b_ring, b_pair = state
        return gather_on_pair(G[c], core * 32, z, col_ring, a_pair), b_ring, b_pair

    def grad_on_ring(c, state):
        a_ring, b_ring, b_pair = state
        b_other = gather_on_ring(G[c], core * 32, z, xh, col_pair, b_ring)
        b_pair.wait_recv()
        return a_ring, b_other, [share(c, z * 8, 8)]

    def grad_part(c, half, copies):
        out = []
        for d, copy in zip(hops, copies):
            copy.wait_recv()
            out.append(share(c, (z + 4 - d) % 4 * 8 + half, 4))
        return out

    def grad_first(c, state):
        a_ring, b_other, cores = state
        return b_other, cores + grad_part(c, 0, a_ring)

    def grad_second(c, state):
        b_other, cores = state
        return cores + grad_part(c, 4, b_other)

    def finish_hidden(c, blocks):
        lanes = slice(c * LANES, (c + 1) * LANES)
        for b in range(4):
            hg_v[b * BLOCK:(b + 1) * BLOCK, lanes] = blocks[b].T.astype(BF16)

    def weight_part(c):
        part = jnp.zeros((LANES, WIDTH), F32)
        for i in range(8):
            for b in range(4):
                pair, ring = i // 4, i % 4
                spot = ring * 4 + pair * 2 + b if b < 2 else 16 + pair * 8 + ring * 2 + b - 2
                nodes = slice((i * 4 + b) * BLOCK, (i * 4 + b + 1) * BLOCK)
                part = part + jnp.dot(PP[c][spot], xg_v[nodes], preferred_element_type=F32)
        part = part.T
        for i in range(8):
            wp[i, c * 48:c * 48 + 32] = part[i * 32:(i + 1) * 32]

    def weight_send():
        return [
            push(wp.at[(row + d) % 8], wr.at[d - 1], ((row + d) % 8, col)) for d in range(1, 8)
        ]

    def weight_cores(copies):
        arrive(copies)
        total = wp[row]
        for d in range(7):
            total = total + wr[d]
        ws[...] = total
        return push(ws.at[pl.ds((1 - core) * 48, 48)], wk, to_core)

    chip = z * 2 + xh

    def weight_chips(copy):
        copy.wait_recv()
        wc[7] = ws[pl.ds(core * 48, 48)] + wk[...]
        out = []
        for d in range(1, 8):
            other = (chip + d) % 8
            out.append(push(wc.at[7], wc.at[d - 1], at(z=other // 2, xh=other % 2)))
        return out

    def weight_back(copies):
        arrive(copies)
        total = wc[(chip + 7) % 8]
        for j in range(1, 8):
            total = total + wc[(chip + 7 - j) % 8]
        mine = pl.ds(core * 48, 48)
        wf[row, mine] = total
        half = wf.at[row, mine]
        return push(half, half, to_core)

    def weight_rows(copy):
        copy.wait_recv()
        mine = wf.at[row]
        return [push(mine, mine, ((row + d) % 8, col)) for d in range(1, 8)]

    def weight_out(copies):
        arrive(copies)
        for c in range(CHUNKS):
            lanes = slice(c * LANES, (c + 1) * LANES)
            n = c * 48
            for i in range(8):
                wg_ref[i * 32:(i + 1) * 32, lanes] = wf[i, n:n + 32] / 256.0
                gg_ref[i * 8:(i + 1) * 8, lanes] = wf[i, n + 32:n + 40] / jnp.sqrt(wf[i, n + 40:n + 48])

    gs0 = gather_start(H[0], 0, y, xl, row_ring, row_pair)
    for load in loads:
        load.start()
    spot = lax.broadcasted_iota(jnp.int32, (1, LANES), 1)
    rows, cols = rows_ref[...], cols_ref[...]
    block = rows % 4
    row_place = (
        rows // 4 % 2 * 32 + rows // 16 * 8 + block // 2 * 4 + rows // 8 % 2 * 2 + block % 2
    )
    block = cols % 4
    col_place = cols // 4 % 4 * 8 + block // 2 * 4 + cols // 16 * 2 + block % 2
    within = spot % 32
    second = within - 16
    ring_at = jnp.where(within < 16, within // 4, second // 2 % 4)
    pair_at = jnp.where(within < 16, within // 2 % 2, second // 8)
    block_at = jnp.where(within < 16, within % 2, 2 + second % 2)
    row_order = ((ring_at * 2 + pair_at) * 2 + spot // 32) * 4 + block_at
    col_order = (pair_at * 4 + ring_at) * 4 + block_at
    live = live_ref[0, 0]
    entries, last = order_slots(rows, col_place, live, 64, row_order)
    table_v[0:1] = entries
    table_v[2:3, 0:LANES] = last
    entries, last = order_slots(cols, row_place, live, 32, col_order)
    table_v[1:2] = entries
    table_v[3:4, 0:LANES] = last
    to_table = pltpu.make_async_copy(table_v, table, t_sem)
    to_table.start()
    ga0 = gather_on_pair(H[0], 0, y, row_ring, gs0[0])
    ids = lax.broadcasted_iota(jnp.int32, (PARTS, 4 * BLOCK), 0)
    mt_v[...] = (part_ref[...] == ids).astype(F32)
    xg_v[pl.ds(row * 512, 512)] = x_ref[...]
    s_v[SLOTS] = jnp.zeros((BLOCK, LANES), BF16)
    gb0 = gather_on_ring(H[0], 0, y, xl, row_pair, gs0[1])
    to_table.wait()
    for load in loads:
        load.wait()
    arrive(ga0 + gb0 + [gs0[2]])
    gs1 = gather_start(H[1], 0, y, xl, row_ring, row_pair)

    acc = tile_pass(0, True, 0, 160, zero)
    ga1 = gather_on_pair(H[1], 0, y, row_ring, gs1[0])
    acc = tile_pass(0, True, 160, 256, acc)
    gb1 = gather_second(H[1], 0, y, xl, row_ring, gs1[2])
    tile_pass(0, True, 256, SLOTS, acc)
    collect(R[0], 2, (1 - core) * 32)
    cs0 = core_send(0)
    collect(R[0], 2, core * 32)
    sizes = jnp.dot(mt_v[...], jnp.ones((4 * BLOCK, LANES), F32), preferred_element_type=F32)
    for c in range(CHUNKS):
        for i in range(8):
            wp[i, c * 48 + 40:c * 48 + 48] = sizes[i * 8:(i + 1) * 8]
    bp0, ar0 = core_start(0, cs0)
    rg_v[...] = lax.dot_general(
        mt_v[...], pg_ref[...], (((0,), (0,)), ((), ())),
        precision=lax.Precision.HIGHEST, preferred_element_type=F32,
    )
    arrive(ga1 + gb1 + gs1[1])
    own_x = xg_v.at[pl.ds(row * 512, 512)]
    rx = [push(own_x, own_x, row_ring(d)) for d in hops]
    acc = tile_pass(1, True, 0, 96, zero)
    br0 = sum_on_pair(COL[0], T[0], z, xh, col_ring, bp0)
    px = push(own_x, own_x, row_pair)
    tile_pass(1, True, 96, SLOTS, acc)
    collect(R[1], 2, (1 - core) * 32)
    cs1 = core_send(1)
    collect(R[1], 2, core * 32)
    ap0 = sum_on_ring(COL[0], T[0], z, xh, col_pair, ar0)
    bp1, ar1 = core_start(1, cs1)
    held0 = activate(0, sum_finish(COL[0], T[0], z, xh, br0, ap0))
    gg0 = grad_start(0)
    br1 = sum_on_pair(COL[1], T[1], z, xh, col_ring, bp1)
    gg0 = grad_on_pair(0, gg0)
    px.wait_recv()
    other_x = xg_v.at[pl.ds(((1 - xl) * 4 + y) * 512, 512)]
    rx += [push(other_x, other_x, row_ring(d)) for d in hops]
    gg0 = grad_on_ring(0, gg0)
    ap1 = sum_on_ring(COL[1], T[1], z, xh, col_pair, ar1)
    after_activate(0, held0)
    held1 = activate(1, sum_finish(COL[1], T[1], z, xh, br1, ap1))
    gg1 = grad_start(1)
    gg0 = grad_first(0, gg0)
    gg1 = grad_on_pair(1, gg1)
    gg0 = grad_second(0, gg0)
    arrive(gg0)
    acc = tile_pass(0, False, 0, 64, zero)
    gg1 = grad_on_ring(1, gg1)
    acc = tile_pass(0, False, 64, 256, acc)
    gg1 = grad_first(1, gg1)
    tile_pass(0, False, 256, SLOTS, acc)
    collect(PP[0], 3, 0)
    bq0, aq0 = row_start(0)
    gg1 = grad_second(1, gg1)
    arrive(rx)
    after_activate(1, held1)
    arrive(gg1)
    acc = tile_pass(1, False, 0, 128, zero)
    dq0 = sum_on_pair(ROW[0], PP[0], y, xl, row_ring, bq0)
    tile_pass(1, False, 128, SLOTS, acc)
    collect(PP[1], 3, 0)
    bq1, aq1 = row_start(1)
    weight_part(1)
    weight_part(0)
    sent = weight_send()
    eq0 = sum_on_ring(ROW[0], PP[0], y, xl, row_pair, aq0)
    dq1 = sum_on_pair(ROW[1], PP[1], y, xl, row_ring, bq1)
    crossed = weight_cores(sent)
    finish_hidden(0, sum_finish(ROW[0], PP[0], y, xl, dq0, eq0))
    passed = weight_chips(crossed)
    eq1 = sum_on_ring(ROW[1], PP[1], y, xl, row_pair, aq1)
    crossed = weight_back(passed)
    passed = weight_rows(crossed)
    finish_hidden(1, sum_finish(ROW[1], PP[1], y, xl, dq1, eq1))
    fg_ref[...] = lax.dot_general(
        hg_v[...], w_ref[...], (((1,), (1,)), ((), ())), preferred_element_type=F32
    ).astype(BF16)
    weight_out(passed)
    for copy in started:
        copy.wait_send()


def hand_over(*refs):
    half = len(refs) // 2
    for src, dst in zip(refs[:half], refs[half:]):
        dst[...] = src[...]


def per_device(
    features, weight, adjacency, block_rows, block_cols, live_blocks, part_gains, partition, cotangent
):
    nodes = features.shape[0]
    smem = pl.BlockSpec(memory_space=pltpu.SMEM)
    vmem = pl.BlockSpec(memory_space=pltpu.VMEM)
    hbm = pl.BlockSpec(memory_space=pl.ANY)

    def pair(shape, dtype=BF16):
        return [pltpu.VMEM(shape, dtype)] * 2

    tile = (BLOCK, LANES)
    sums = [
        *pair((3, 4) + tile), *pair((8,) + tile), *pair((8,) + tile),
        *pair((3, 2) + tile), *pair((2,) + tile), *pair((2,) + tile),
    ]
    copies = 2 * 55 + 7 + 23
    outs = (
        jax.ShapeDtypeStruct((nodes, WIDTH), BF16),
        jax.ShapeDtypeStruct((nodes, WIDTH), BF16),
        jax.ShapeDtypeStruct((WIDTH, WIDTH), F32),
        jax.ShapeDtypeStruct((PARTS, WIDTH), F32),
    )
    results = pl.pallas_call(
        kernel,
        out_shape=outs,
        in_specs=[vmem, vmem, smem, vmem, vmem, hbm, vmem, vmem, vmem],
        out_specs=(vmem,) * 4,
        scratch_shapes=[
            pltpu.VMEM((8, SLOTS), jnp.int32),
            pltpu.SMEM((8, SLOTS), jnp.int32),
            pltpu.VMEM((SLOTS,) + tile, BF16),
            pltpu.VMEM((SLOTS + 1,) + tile, BF16),
            *pair((32,) + tile), *pair((64,) + tile), *pair((32,) + tile), *pair((32,) + tile),
            *pair((64,) + tile), *pair((32,) + tile),
            *sums, *sums,
            pltpu.VMEM((8, 96, LANES), F32), pltpu.VMEM((7, 96, LANES), F32),
            pltpu.VMEM((96, LANES), F32), pltpu.VMEM((48, LANES), F32),
            pltpu.VMEM((8, 48, LANES), F32), pltpu.VMEM((8, 96, LANES), F32),
            pltpu.VMEM((nodes, WIDTH), F32),
            pltpu.VMEM((PARTS, nodes), F32),
            pltpu.VMEM((8 * nodes, WIDTH), BF16),
            pltpu.VMEM((nodes, WIDTH), BF16),
            pltpu.SemaphoreType.DMA((4,)),
            pltpu.SemaphoreType.DMA,
            pltpu.SemaphoreType.DMA((copies,)),
            pltpu.SemaphoreType.DMA((copies,)),
        ],
        compiler_params=pltpu.CompilerParams(
            collective_id=0, has_side_effects=True, vmem_limit_bytes=60 * 2**20
        ),
    )(
        block_rows.reshape(1, SLOTS), block_cols.reshape(1, SLOTS), live_blocks,
        features, weight, adjacency[0, 0], part_gains, partition.reshape(1, nodes), cotangent,
    )
    return pl.pallas_call(
        hand_over,
        out_shape=outs,
        in_specs=[vmem] * 4,
        out_specs=(vmem,) * 4,
    )(*results)


def solution(mesh):
    in_specs = (
        P(("row", "col"), None),
        P(),
        P("row", "col", None, None, None),
        P("row", "col", None),
        P("row", "col", None),
        P("row", "col"),
        P(),
        P(("row", "col")),
        P(("row", "col"), None),
    )
    out_specs = (P(("row", "col"), None), P(("row", "col"), None), P(), P())
    return jax.shard_map(
        per_device, mesh=mesh, in_specs=in_specs, out_specs=out_specs, check_vma=False
    )
```

```python
import jax
import jax.numpy as jnp
from jax import lax
from jax.experimental import pallas as pl
from jax.experimental.pallas import tpu as pltpu
from jax.sharding import PartitionSpec as P

BLOCK = 128
SLOTS = 384
WIDTH = 256
CHUNKS = 2
LANES = 128
PARTS = 64
NODES = 65536
UNROLL = 32
MESH = pl.DeviceIdType.MESH
F32 = jnp.float32
BF16 = jnp.bfloat16


def order_slots(target, other, live_count, count, order):
    slot = lax.broadcasted_iota(jnp.int32, (1, SLOTS), 1)

    def column(row):
        return jnp.broadcast_to(row, (LANES, SLOTS)).T

    def wide(tall):
        return jnp.concatenate([tall] * (SLOTS // LANES), axis=1)

    def total(flags):
        return jnp.sum(flags.astype(jnp.int32), axis=0, keepdims=True)

    key = jnp.where(slot < live_count, target, count)
    mark = key * 512 + slot
    key_col = column(key)
    mark_col = wide(column(mark))
    rank = total(mark_col < mark)
    below = total(mark_col < key * 512)
    keep = (rank != below).astype(jnp.int32)
    entry = wide(column((slot * 64 + other) * 2 + keep))
    hit = wide(column(rank)) == slot
    entries = jnp.sum(jnp.where(hit, entry, 0), axis=0, keepdims=True)
    upto = total(key_col <= order)
    some = total(key_col == order)
    return entries, jnp.where(some > 0, upto - 1, SLOTS)


def silu_parts(v):
    g = 1.0 / (1.0 + jnp.exp(-v))
    return v * g, g * (1.0 + v * (1.0 - g))


def kernel(
    rows_ref, cols_ref, live_ref, x_ref, w_ref, a_hbm, pg_ref, part_ref, cot_ref,
    lo_ref, fg_ref, wg_ref, gg_ref,
    table_v, table, a_v, s_v, h0, h1, r0, r1, cx0, cx1, t0, t1, g0, g1, p0, p1,
    ca0, ca1, cp0, cp1, cm0, cm1, cb0, cb1, cs0_, cs1_, cl0, cl1,
    ra0, ra1, rp0, rp1, rm0, rm1, rb0, rb1, rs0_, rs1_, rl0, rl1,
    wp, wr, ws, wk, wc, wf,
    rg_v, mt_v, xg_v, hg_v,
    a_sem, t_sem, send, recv,
):
    row = lax.axis_index("row")
    col = lax.axis_index("col")
    xl, y = row // 4, row % 4
    z, xh, core = col // 4, (col // 2) % 2, col % 2

    def at(xl=xl, y=y, z=z, xh=xh, core=core):
        return (xl * 4 + y, z * 4 + xh * 2 + core)

    H, R, CX, T, G, PP = (h0, h1), (r0, r1), (cx0, cx1), (t0, t1), (g0, g1), (p0, p1)
    COL = ((ca0, cp0, cm0, cb0, cs0_, cl0), (ca1, cp1, cm1, cb1, cs1_, cl1))
    ROW = ((ra0, rp0, rm0, rb0, rs0_, rl0), (ra1, rp1, rm1, rb1, rs1_, rl1))

    started = []

    def push(src, dst, device):
        n = len(started)
        copy = pltpu.make_async_remote_copy(
            src_ref=src, dst_ref=dst, send_sem=send.at[n], recv_sem=recv.at[n],
            device_id=device, device_id_type=MESH,
        )
        copy.start()
        started.append(copy)
        return copy

    def arrive(copies):
        for copy in copies:
            copy.wait_recv()

    pieces = 4
    step = SLOTS // pieces
    loads = [
        pltpu.make_async_copy(
            a_hbm.at[pl.ds(n * step, step)], a_v.at[pl.ds(n * step, step)], a_sem.at[n]
        )
        for n in range(pieces)
    ]

    barrier = pltpu.get_barrier_semaphore()
    near = [at(xl=1 - xl), at(xh=1 - xh), at(core=1 - core)]
    near += [at(y=(y + d) % 4) for d in (1, 3, 2)] + [at(z=(z + d) % 4) for d in (1, 3, 2)]
    for device in near:
        pl.semaphore_signal(barrier, inc=1, device_id=device, device_id_type=MESH)

    for c in range(CHUNKS):
        hidden = jnp.dot(x_ref[...], w_ref[:, c * LANES:(c + 1) * LANES], preferred_element_type=F32)
        hidden = hidden.astype(BF16).reshape(4, BLOCK, LANES)
        H[c][pl.ds(y * 8 + xl * 2, 2)] = hidden[0:2]
        H[c][pl.ds(y * 8 + 4 + xl * 2, 2)] = hidden[2:4]
    pl.semaphore_wait(barrier, 9)

    row_ring, row_pair = (lambda d: at(y=(y + d) % 4)), at(xl=1 - xl)
    col_ring, col_pair = (lambda d: at(z=(z + d) % 4)), at(xh=1 - xh)
    hops = (1, 3, 2)

    def gather_start(buf, base, ring, pair, to_ring, to_pair):
        first = buf.at[pl.ds(base + ring * 8 + pair * 2, 2)]
        second = buf.at[pl.ds(base + ring * 8 + 4 + pair * 2, 2)]
        a_pair = push(first, first, to_pair)
        b_ring = [push(second, second, to_ring(d)) for d in hops]
        return a_pair, b_ring, push(second, second, to_pair)

    def gather_on_pair(buf, base, ring, to_ring, a_pair):
        a_pair.wait_recv()
        both = buf.at[pl.ds(base + ring * 8, 4)]
        return [push(both, both, to_ring(d)) for d in hops]

    def gather_on_ring(buf, base, ring, pair, to_pair, b_ring):
        out = []
        for d, copy in zip(hops, b_ring):
            copy.wait_recv()
            got = buf.at[pl.ds(base + (ring + 4 - d) % 4 * 8 + 4 + pair * 2, 2)]
            out.append(push(got, got, to_pair))
        return out

    def gather_second(buf, base, ring, pair, to_ring, b_pair):
        b_pair.wait_recv()
        other = buf.at[pl.ds(base + ring * 8 + 4 + (1 - pair) * 2, 2)]
        return [push(other, other, to_ring(d)) for d in hops]

    def sum_start_pair(bufs, src, ring, pair, to_pair):
        b_pair = []
        for d in (2, 1, 3, 0):
            spot = (ring + d) % 4 * 2
            b_pair.append(
                push(src.at[pl.ds(16 + (1 - pair) * 8 + spot, 2)], bufs[1].at[pl.ds(spot, 2)], to_pair)
            )
        return b_pair

    def sum_start_ring(bufs, src, ring, to_ring):
        return [
            push(src.at[pl.ds(((ring + d) % 4) * 4, 4)], bufs[0].at[d - 1], to_ring(d)) for d in hops
        ]

    def row_start(c):
        b_pair = sum_start_pair(ROW[c], PP[c], y, xl, row_pair)
        return b_pair, sum_start_ring(ROW[c], PP[c], y, row_ring)

    def sum_on_pair(bufs, src, ring, pair, to_ring, b_pair):
        out = []
        for d, copy in zip((2, 1, 3), b_pair):
            copy.wait_recv()
            spot = pl.ds((ring + d) % 4 * 2, 2)
            mine = src[pl.ds(16 + pair * 8 + (ring + d) % 4 * 2, 2)]
            bufs[2][spot] = (mine.astype(F32) + bufs[1][spot].astype(F32)).astype(BF16)
            out.append(push(bufs[2].at[spot], bufs[3].at[d - 1], to_ring(d)))
        return out, b_pair[3]

    def first_half(bufs, src, ring, which):
        total = src[pl.ds(ring * 4 + which * 2, 2)].astype(F32)
        for d in range(3):
            total = total + bufs[0][d, pl.ds(which * 2, 2)].astype(F32)
        return total

    def sum_on_ring(bufs, src, ring, pair, to_pair, a_ring):
        arrive(a_ring)
        bufs[4][...] = first_half(bufs, src, ring, 1 - pair).astype(BF16)
        return push(bufs[4], bufs[5], to_pair)

    def sum_finish(bufs, src, ring, pair, on_pair, a_pair):
        b_ring, b_own = on_pair
        b_own.wait_recv()
        arrive(b_ring)
        second = src[pl.ds(16 + pair * 8 + ring * 2, 2)].astype(F32)
        second = second + bufs[1][pl.ds(ring * 2, 2)].astype(F32)
        for d in range(3):
            second = second + bufs[3][d].astype(F32)
        a_pair.wait_recv()
        first = first_half(bufs, src, ring, pair) + bufs[5][...].astype(F32)
        return first[0], first[1], second[0], second[1]

    def tile_pass(c, forward, first, stop, acc):
        line = 0 if forward else 1
        panels = (H if forward else G)[c]

        def body(t, acc):
            for u in range(UNROLL):
                k = t * UNROLL + u
                entry = table[line, k]
                block = a_v[entry >> 7]
                panel = panels[(entry >> 1) & 63]
                if forward:
                    term = jnp.dot(block, panel, preferred_element_type=F32)
                else:
                    term = jnp.dot(panel, block, preferred_element_type=F32)
                acc = acc * (entry & 1).astype(F32) + term
                s_v[k] = acc.astype(BF16)
            return acc

        return lax.fori_loop(first // UNROLL, stop // UNROLL, body, acc)

    def collect(dst, line, first):
        def body(q, carry):
            for u in range(8):
                b = first + q * 8 + u
                dst[b] = s_v[table[line, b]]
            return carry

        lax.fori_loop(0, 4, body, 0)

    zero = jnp.zeros((BLOCK, LANES), F32)

    core_order = (16 + (1 - xh) * 8, 0, 8, 16 + xh * 8)

    def core_send(c):
        return [
            push(R[c].at[pl.ds((1 - core) * 32 + n, 8)], CX[c].at[pl.ds(n, 8)], at(core=1 - core))
            for n in core_order
        ]

    def core_add(c, copies, parts):
        for p in parts:
            copies[p].wait_recv()
            for u in range(8):
                b = core_order[p] + u
                T[c][b] = (R[c][core * 32 + b].astype(F32) + CX[c][b].astype(F32)).astype(BF16)

    def core_start(c, copies):
        core_add(c, copies, (0,))
        b_pair = sum_start_pair(COL[c], T[c], z, xh, col_pair)
        core_add(c, copies, (1, 2))
        a_ring = sum_start_ring(COL[c], T[c], z, col_ring)
        core_add(c, copies, (3,))
        return b_pair, a_ring

    def activate(c, blocks):
        lanes = slice(c * LANES, (c + 1) * LANES)
        held = []
        for b in range(4):
            nodes = slice(b * BLOCK, (b + 1) * BLOCK)
            act, slope = silu_parts(blocks[b])
            cot = cot_ref[nodes, lanes].astype(F32)
            grad = cot * rg_v[nodes, lanes] * slope
            G[c][core * 32 + z * 8 + b // 2 * 4 + xh * 2 + b % 2] = grad.T.astype(BF16)
            held.append(act)
        return held

    def after_activate(c, held):
        lanes = slice(c * LANES, (c + 1) * LANES)
        act = jnp.concatenate(held, axis=0)
        lo_ref[:, lanes] = (act * rg_v[:, lanes]).astype(BF16)
        terms = jnp.dot(
            mt_v[...], cot_ref[:, lanes].astype(F32) * act,
            precision=lax.Precision.HIGHEST, preferred_element_type=F32,
        )
        for i in range(8):
            wp[i, c * 48 + 32:c * 48 + 40] = terms[i * 8:(i + 1) * 8]

    to_core = at(core=1 - core)

    def share(c, first, count):
        got = G[c].at[pl.ds(core * 32 + first, count)]
        return push(got, got, to_core)

    def grad_start(c):
        return gather_start(G[c], core * 32, z, xh, col_ring, col_pair)

    def grad_on_pair(c, state):
        a_pair, b_ring, b_pair = state
        return gather_on_pair(G[c], core * 32, z, col_ring, a_pair), b_ring, b_pair

    def grad_on_ring(c, state):
        a_ring, b_ring, b_pair = state
        b_other = gather_on_ring(G[c], core * 32, z, xh, col_pair, b_ring)
        b_pair.wait_recv()
        return a_ring, b_other, [share(c, z * 8, 8)]

    def grad_on_ring_light(c, state):
        a_ring, b_ring, b_pair = state
        b_other = gather_second(G[c], core * 32, z, xh, col_ring, b_pair)
        cores = [share(c, z * 8, 8)]
        arrive(b_ring)
        return a_ring, b_other, cores

    def grad_part(c, half, copies):
        out = []
        for d, copy in zip(hops, copies):
            copy.wait_recv()
            out.append(share(c, (z + 4 - d) % 4 * 8 + half, 4))
        return out

    def grad_first(c, state):
        a_ring, b_other, cores = state
        return b_other, cores + grad_part(c, 0, a_ring)

    def grad_second(c, state):
        b_other, cores = state
        return cores + grad_part(c, 4, b_other)

    def finish_hidden(c, blocks):
        lanes = slice(c * LANES, (c + 1) * LANES)
        for b in range(4):
            hg_v[b * BLOCK:(b + 1) * BLOCK, lanes] = blocks[b].T.astype(BF16)

    def weight_part(c):
        part = jnp.zeros((LANES, WIDTH), F32)
        for i in range(8):
            for b in range(4):
                pair, ring = i // 4, i % 4
                spot = ring * 4 + pair * 2 + b if b < 2 else 16 + pair * 8 + ring * 2 + b - 2
                nodes = slice((i * 4 + b) * BLOCK, (i * 4 + b + 1) * BLOCK)
                part = part + jnp.dot(PP[c][spot], xg_v[nodes], preferred_element_type=F32)
        part = part.T
        for i in range(8):
            wp[i, c * 48:c * 48 + 32] = part[i * 32:(i + 1) * 32]

    def weight_send():
        return [
            push(wp.at[(row + d) % 8], wr.at[d - 1], ((row + d) % 8, col)) for d in range(1, 8)
        ]

    def weight_cores(copies):
        arrive(copies)
        total = wp[row]
        for d in range(7):
            total = total + wr[d]
        ws[...] = total
        return push(ws.at[pl.ds((1 - core) * 48, 48)], wk, to_core)

    chip = z * 2 + xh

    def weight_chips(copy):
        copy.wait_recv()
        wc[7] = ws[pl.ds(core * 48, 48)] + wk[...]
        out = []
        for d in range(1, 8):
            other = (chip + d) % 8
            out.append(push(wc.at[7], wc.at[d - 1], at(z=other // 2, xh=other % 2)))
        return out

    def weight_back(copies):
        arrive(copies)
        total = wc[(chip + 7) % 8]
        for j in range(1, 8):
            total = total + wc[(chip + 7 - j) % 8]
        mine = pl.ds(core * 48, 48)
        wf[row, mine] = total
        half = wf.at[row, mine]
        return push(half, half, to_core)

    def weight_rows(copy):
        copy.wait_recv()
        mine = wf.at[row]
        return [push(mine, mine, ((row + d) % 8, col)) for d in range(1, 8)]

    def weight_out(copies):
        arrive(copies)
        for c in range(CHUNKS):
            lanes = slice(c * LANES, (c + 1) * LANES)
            n = c * 48
            for i in range(8):
                wg_ref[i * 32:(i + 1) * 32, lanes] = wf[i, n:n + 32] / 256.0
                gg_ref[i * 8:(i + 1) * 8, lanes] = wf[i, n + 32:n + 40] / jnp.sqrt(wf[i, n + 40:n + 48])

    gs0 = gather_start(H[0], 0, y, xl, row_ring, row_pair)
    for load in loads:
        load.start()
    spot = lax.broadcasted_iota(jnp.int32, (1, LANES), 1)
    rows, cols = rows_ref[...], cols_ref[...]
    block = rows % 4
    row_place = (
        rows // 4 % 2 * 32 + rows // 16 * 8 + block // 2 * 4 + rows // 8 % 2 * 2 + block % 2
    )
    block = cols % 4
    col_place = cols // 4 % 4 * 8 + block // 2 * 4 + cols // 16 * 2 + block % 2
    within = spot % 32
    second = within - 16
    ring_at = jnp.where(within < 16, within // 4, second // 2 % 4)
    pair_at = jnp.where(within < 16, within // 2 % 2, second // 8)
    block_at = jnp.where(within < 16, within % 2, 2 + second % 2)
    row_order = ((ring_at * 2 + pair_at) * 2 + spot // 32) * 4 + block_at
    col_order = (pair_at * 4 + ring_at) * 4 + block_at
    live = live_ref[0, 0]
    entries, last = order_slots(rows, col_place, live, 64, row_order)
    table_v[0:1] = entries
    table_v[2:3, 0:LANES] = last
    entries, last = order_slots(cols, row_place, live, 32, col_order)
    table_v[1:2] = entries
    table_v[3:4, 0:LANES] = last
    to_table = pltpu.make_async_copy(table_v, table, t_sem)
    to_table.start()
    ga0 = gather_on_pair(H[0], 0, y, row_ring, gs0[0])
    ids = lax.broadcasted_iota(jnp.int32, (PARTS, 4 * BLOCK), 0)
    mt_v[...] = (part_ref[...] == ids).astype(F32)
    xg_v[pl.ds(row * 512, 512)] = x_ref[...]
    s_v[SLOTS] = jnp.zeros((BLOCK, LANES), BF16)
    gb0 = gather_on_ring(H[0], 0, y, xl, row_pair, gs0[1])
    to_table.wait()
    for load in loads:
        load.wait()
    arrive(ga0 + gb0 + [gs0[2]])
    gs1 = gather_start(H[1], 0, y, xl, row_ring, row_pair)

    acc = tile_pass(0, True, 0, 160, zero)
    ga1 = gather_on_pair(H[1], 0, y, row_ring, gs1[0])
    acc = tile_pass(0, True, 160, 256, acc)
    gb1 = gather_second(H[1], 0, y, xl, row_ring, gs1[2])
    tile_pass(0, True, 256, SLOTS, acc)
    collect(R[0], 2, (1 - core) * 32)
    cs0 = core_send(0)
    collect(R[0], 2, core * 32)
    sizes = jnp.dot(mt_v[...], jnp.ones((4 * BLOCK, LANES), F32), preferred_element_type=F32)
    for c in range(CHUNKS):
        for i in range(8):
            wp[i, c * 48 + 40:c * 48 + 48] = sizes[i * 8:(i + 1) * 8]
    bp0, ar0 = core_start(0, cs0)
    rg_v[...] = lax.dot_general(
        mt_v[...], pg_ref[...], (((0,), (0,)), ((), ())),
        precision=lax.Precision.HIGHEST, preferred_element_type=F32,
    )
    arrive(ga1 + gb1 + gs1[1])
    own_x = xg_v.at[pl.ds(row * 512, 512)]
    rx = [push(own_x, own_x, row_ring(d)) for d in hops]
    acc = tile_pass(1, True, 0, 96, zero)
    br0 = sum_on_pair(COL[0], T[0], z, xh, col_ring, bp0)
    px = push(own_x, own_x, row_pair)
    tile_pass(1, True, 96, SLOTS, acc)
    collect(R[1], 2, (1 - core) * 32)
    cs1 = core_send(1)
    collect(R[1], 2, core * 32)
    ap0 = sum_on_ring(COL[0], T[0], z, xh, col_pair, ar0)
    bp1, ar1 = core_start(1, cs1)
    held0 = activate(0, sum_finish(COL[0], T[0], z, xh, br0, ap0))
    gg0 = grad_start(0)
    br1 = sum_on_pair(COL[1], T[1], z, xh, col_ring, bp1)
    gg0 = grad_on_pair(0, gg0)
    px.wait_recv()
    other_x = xg_v.at[pl.ds(((1 - xl) * 4 + y) * 512, 512)]
    rx += [push(other_x, other_x, row_ring(d)) for d in hops]
    gg0 = grad_on_ring(0, gg0)
    ap1 = sum_on_ring(COL[1], T[1], z, xh, col_pair, ar1)
    after_activate(0, held0)
    held1 = activate(1, sum_finish(COL[1], T[1], z, xh, br1, ap1))
    gg1 = grad_start(1)
    gg0 = grad_first(0, gg0)
    gg1 = grad_on_pair(1, gg1)
    gg0 = grad_second(0, gg0)
    arrive(gg0)
    acc = tile_pass(0, False, 0, 64, zero)
    gg1 = grad_on_ring_light(1, gg1)
    acc = tile_pass(0, False, 64, 256, acc)
    gg1 = grad_first(1, gg1)
    tile_pass(0, False, 256, SLOTS, acc)
    collect(PP[0], 3, 0)
    bq0, aq0 = row_start(0)
    gg1 = grad_second(1, gg1)
    arrive(rx)
    after_activate(1, held1)
    arrive(gg1)
    acc = tile_pass(1, False, 0, 128, zero)
    dq0 = sum_on_pair(ROW[0], PP[0], y, xl, row_ring, bq0)
    tile_pass(1, False, 128, SLOTS, acc)
    collect(PP[1], 3, 0)
    bq1, aq1 = row_start(1)
    weight_part(1)
    weight_part(0)
    sent = weight_send()
    eq0 = sum_on_ring(ROW[0], PP[0], y, xl, row_pair, aq0)
    dq1 = sum_on_pair(ROW[1], PP[1], y, xl, row_ring, bq1)
    crossed = weight_cores(sent)
    finish_hidden(0, sum_finish(ROW[0], PP[0], y, xl, dq0, eq0))
    passed = weight_chips(crossed)
    eq1 = sum_on_ring(ROW[1], PP[1], y, xl, row_pair, aq1)
    crossed = weight_back(passed)
    passed = weight_rows(crossed)
    finish_hidden(1, sum_finish(ROW[1], PP[1], y, xl, dq1, eq1))
    fg_ref[...] = lax.dot_general(
        hg_v[...], w_ref[...], (((1,), (1,)), ((), ())), preferred_element_type=F32
    ).astype(BF16)
    weight_out(passed)
    for copy in started:
        copy.wait_send()


def hand_over(*refs):
    half = len(refs) // 2
    for src, dst in zip(refs[:half], refs[half:]):
        dst[...] = src[...]


def per_device(
    features, weight, adjacency, block_rows, block_cols, live_blocks, part_gains, partition, cotangent
):
    nodes = features.shape[0]
    smem = pl.BlockSpec(memory_space=pltpu.SMEM)
    vmem = pl.BlockSpec(memory_space=pltpu.VMEM)
    hbm = pl.BlockSpec(memory_space=pl.ANY)

    def pair(shape, dtype=BF16):
        return [pltpu.VMEM(shape, dtype)] * 2

    tile = (BLOCK, LANES)
    sums = [
        *pair((3, 4) + tile), *pair((8,) + tile), *pair((8,) + tile),
        *pair((3, 2) + tile), *pair((2,) + tile), *pair((2,) + tile),
    ]
    copies = 2 * 55 + 7 + 23
    outs = (
        jax.ShapeDtypeStruct((nodes, WIDTH), BF16),
        jax.ShapeDtypeStruct((nodes, WIDTH), BF16),
        jax.ShapeDtypeStruct((WIDTH, WIDTH), F32),
        jax.ShapeDtypeStruct((PARTS, WIDTH), F32),
    )
    results = pl.pallas_call(
        kernel,
        out_shape=outs,
        in_specs=[vmem, vmem, smem, vmem, vmem, hbm, vmem, vmem, vmem],
        out_specs=(vmem,) * 4,
        scratch_shapes=[
            pltpu.VMEM((8, SLOTS), jnp.int32),
            pltpu.SMEM((8, SLOTS), jnp.int32),
            pltpu.VMEM((SLOTS,) + tile, BF16),
            pltpu.VMEM((SLOTS + 1,) + tile, BF16),
            *pair((32,) + tile), *pair((64,) + tile), *pair((32,) + tile), *pair((32,) + tile),
            *pair((64,) + tile), *pair((32,) + tile),
            *sums, *sums,
            pltpu.VMEM((8, 96, LANES), F32), pltpu.VMEM((7, 96, LANES), F32),
            pltpu.VMEM((96, LANES), F32), pltpu.VMEM((48, LANES), F32),
            pltpu.VMEM((8, 48, LANES), F32), pltpu.VMEM((8, 96, LANES), F32),
            pltpu.VMEM((nodes, WIDTH), F32),
            pltpu.VMEM((PARTS, nodes), F32),
            pltpu.VMEM((8 * nodes, WIDTH), BF16),
            pltpu.VMEM((nodes, WIDTH), BF16),
            pltpu.SemaphoreType.DMA((4,)),
            pltpu.SemaphoreType.DMA,
            pltpu.SemaphoreType.DMA((copies,)),
            pltpu.SemaphoreType.DMA((copies,)),
        ],
        compiler_params=pltpu.CompilerParams(
            collective_id=0, has_side_effects=True, vmem_limit_bytes=60 * 2**20
        ),
    )(
        block_rows.reshape(1, SLOTS), block_cols.reshape(1, SLOTS), live_blocks,
        features, weight, adjacency[0, 0], part_gains, partition.reshape(1, nodes), cotangent,
    )
    return pl.pallas_call(
        hand_over,
        out_shape=outs,
        in_specs=[vmem] * 4,
        out_specs=(vmem,) * 4,
    )(*results)


def solution(mesh):
    in_specs = (
        P(("row", "col"), None),
        P(),
        P("row", "col", None, None, None),
        P("row", "col", None),
        P("row", "col", None),
        P("row", "col"),
        P(),
        P(("row", "col")),
        P(("row", "col"), None),
    )
    out_specs = (P(("row", "col"), None), P(("row", "col"), None), P(), P())
    return jax.shard_map(
        per_device, mesh=mesh, in_specs=in_specs, out_specs=out_specs, check_vma=False
    )
```
